32 devices in a mesh: gx: 8 (over z, y), gy: 4 (over x, core).
Axes of the slice: x: 2, y: 2, z: 4, core: 2. Of those that a mesh axis runs over, the one named last changes fastest.
Arguments:
- tokens: bfloat16 [48, 24, 8, 384], P('gx', 'gy'), may hold values from -6 to 6
- upstream: bfloat16 [48, 24, 8, 384], P('gx', 'gy'), may hold values from -41 to 41
- window_labels: int32 [48, 24, 8], P('gx', 'gy'), may hold values from 0 to 2
- ln1_gain: float32 [384], replicated, may hold values from 0.5 to 1.5
- w_qkv: bfloat16 [384, 1152], replicated, as said below
- w_proj: bfloat16 [384, 384], replicated, may hold values from -0.3125 to 0.3125
- ln2_gain: float32 [384], replicated, may hold values from 0.5 to 1.5
- w_fc1: bfloat16 [384, 1536], replicated, may hold values from -0.3125 to 0.3125
- b_fc1: float32 [1536], replicated, may hold values from -3 to 3
- w_fc2: bfloat16 [1536, 384], replicated, may hold values from -0.15625 to 0.15625
Outputs:
- d_tokens: bfloat16 [48, 24, 8, 384], P('gx', 'gy')
- g_ln1: float32 [384], replicated
- g_qkv: bfloat16 [384, 1152], replicated
- g_proj: bfloat16 [384, 384], replicated
- g_ln2: float32 [384], replicated
- g_fc1: bfloat16 [384, 1536], replicated
- g_bfc1: float32 [1536], replicated
- g_fc2: bfloat16 [1536, 384], replicated
The draws below stay inside these ranges and needn't reach their ends.
Inputs may be any that keep to these rules, and one draw needn't show every extreme that they name: `w_qkv`: entries at most 28 / sqrt(384) in magnitude.
All inputs are finite; a program needn't handle non-finite values.
Results may differ from the reference program's by a relative error of at most 0.019.
Values may be sent and summed in bfloat16 or wider, within the bound.
No kernel may reach another device: no remote copies, remote signals or barrier semaphores. Data moves between devices by JAX's collectives and lax.ppermute only.
A program may use at most 128 MiB of HBM per device.

```python
import math
import jax
import jax.numpy as jnp
from jax import lax

HD = 32
D = 384
FF = 1536
WX = 6
WY = 6
WZ = 8
NX = 48
NY = 24
NZ = 8


def draw_upstream(key, part):
    key_base, key_tok, key_col = jax.random.split(key, 3)
    shape = (NX, NY, NZ, D)
    ramp_x = jnp.arange(NX, dtype=jnp.float32) / max(NX - 1, 1)
    ramp_y = jnp.arange(NY, dtype=jnp.float32) / max(NY - 1, 1)
    ramp = jnp.exp(0.5 * math.log(3.0) * (ramp_x[:, None] + ramp_y[None, :]))[:, :, None, None]
    token_scale = jnp.exp(jax.random.uniform(key_tok, (NX, NY, NZ, 1), minval=0.0, maxval=math.log(3.0)))
    column_scale = jnp.exp(jax.random.uniform(key_col, (D,), minval=0.0, maxval=math.log(3.0)))
    base = jnp.clip(jax.random.normal(key_base, shape), -6.0, 6.0)
    return (0.25 * base * ramp * token_scale * column_scale).astype(jnp.bfloat16)


def draw_w_qkv(key, part):
    key_base = jax.random.fold_in(key, 0)
    base = jnp.clip(jax.random.normal(key_base, (D, 3 * D)), -4.0, 4.0) / math.sqrt(D)
    return base.astype(jnp.bfloat16)


def touch_ends(result, stream_key, low, largest):
    spot = [jax.random.randint(jax.random.fold_in(stream_key, axis), (), 0, length) for axis, length in enumerate(result.shape)]
    main_axis = result.shape.index(max(result.shape))
    beside = spot[:main_axis] + [(spot[main_axis] + 1) % result.shape[main_axis]] + spot[main_axis + 1:]
    return result.at[tuple(spot)].set(low).at[tuple(beside)].set(largest)


def block_scale(stream_key, extent, shards, smallest, high):
    def one(dim, parts):
        draws = jax.random.uniform(jax.random.fold_in(jax.random.fold_in(stream_key, 6), dim), (parts,), jnp.float32, smallest / len(shards), high / len(shards))
        return jnp.repeat(jnp.exp(draws), extent[dim] // parts).reshape((-1,) + (1,) * (len(extent) - dim - 1))

    loudness = one(*shards[0])
    for cut in shards[1:]:
        loudness = loudness * one(*cut)
    return loudness


def normal_values(own_key, shape, deviation, limit, pieces=(), kind=jnp.bfloat16):
    drawn = deviation * jax.random.normal(own_key, shape, jnp.float32)
    if pieces:
        drawn = drawn * block_scale(own_key, shape, pieces, -0.22, 0.18)
    return jnp.clip(drawn, -limit, limit).astype(kind)


def setup_inputs(seed: int = 0) -> dict:
    arg_keys = jax.random.split(jax.random.key(seed), 11)
    return {
        "tokens": normal_values(arg_keys[0], (NX, NY, NZ, D), 1.0, 6.0, ((0, 8), (1, 4))),
        "upstream": draw_upstream(jax.random.fold_in(arg_keys[10], 71), 0),
        "window_labels": touch_ends(jax.random.randint(arg_keys[2], (NX, NY, NZ), 0, 3), jax.random.fold_in(arg_keys[2], 1), 0, 2).astype(jnp.int32),
        "ln1_gain": jnp.clip(1.0 + 0.1 * jax.random.normal(arg_keys[3], (D,), jnp.float32), 0.5, 1.5),
        "w_qkv": draw_w_qkv(jax.random.fold_in(arg_keys[10], 71), 0),
        "w_proj": normal_values(arg_keys[5], (D, D), D ** -0.5, 0.3125),
        "ln2_gain": jnp.clip(1.0 + 0.1 * jax.random.normal(arg_keys[6], (D,), jnp.float32), 0.5, 1.5),
        "w_fc1": normal_values(arg_keys[7], (D, FF), D ** -0.5, 0.3125),
        "b_fc1": normal_values(arg_keys[8], (FF,), 0.5, 3.0, (), jnp.float32),
        "w_fc2": normal_values(arg_keys[9], (FF, D), FF ** -0.5, 0.15625),
    }


EPS = 1e-05
CUBIC = 0.044715
ROOT_TWO_PI = math.sqrt(2.0 / math.pi)

def row_stats(values):
    row_mean = lax.optimization_barrier(jnp.mean(values, axis=-1, keepdims=True))
    center = values - row_mean
    variance = lax.optimization_barrier(jnp.mean(center * center, axis=-1, keepdims=True))
    inv_std = lax.rsqrt(variance + EPS)
    return (center * inv_std, inv_std)

def norm_back(incoming, normed, inv_std, gain_vec):
    scaled = incoming * gain_vec
    first_mean = lax.optimization_barrier(jnp.mean(scaled, axis=-1, keepdims=True))
    second_mean = lax.optimization_barrier(jnp.mean(scaled * normed, axis=-1, keepdims=True))
    flat_terms = (incoming * normed).reshape(-1, incoming.shape[-1])
    return (inv_std * (scaled - first_mean - normed * second_mean), lax.optimization_barrier(jnp.sum(flat_terms, axis=0)))

def gelu_pair(preact):
    cubic_arg = ROOT_TWO_PI * (preact + CUBIC * preact * preact * preact)
    tanh_value = jnp.tanh(cubic_arg)
    gelu_value = 0.5 * preact * (1.0 + tanh_value)
    gelu_slope = 0.5 * (1.0 + tanh_value) + 0.5 * preact * (1.0 - tanh_value * tanh_value) * ROOT_TWO_PI * (1.0 + 3.0 * CUBIC * preact * preact)
    return (gelu_value, gelu_slope)

def to_windows(grid_tile, win_depth):
    tile_x, tile_y, tile_z = grid_tile.shape[:3]
    trailing = grid_tile.shape[3:]
    blocks = tile_z // win_depth
    shaped = grid_tile.reshape((tile_x, tile_y, blocks, win_depth) + trailing)
    axes_order = (2, 0, 1, 3) + tuple(range(4, 4 + len(trailing)))
    return shaped.transpose(axes_order).reshape((blocks, tile_x * tile_y * win_depth) + trailing)

def from_windows(win_rows, tile_x, tile_y, win_depth):
    blocks = win_rows.shape[0]
    trailing = win_rows.shape[2:]
    shaped = win_rows.reshape((blocks, tile_x, tile_y, win_depth) + trailing)
    axes_order = (1, 2, 0, 3) + tuple(range(4, 4 + len(trailing)))
    return shaped.transpose(axes_order).reshape((tile_x, tile_y, blocks * win_depth) + trailing)

def block_grads(wide_rows, up_rows, region_codes, ln1_gain, w_qkv, w_proj, ln2_gain, w_fc1, b_fc1, w_fc2):
    blocks, length, model_width = wide_rows.shape
    head_count = model_width // HD
    score_scale = HD ** (-0.5)
    normed_first, inv_first = row_stats(wide_rows)
    h_rows = (normed_first * ln1_gain).astype(jnp.bfloat16)
    packed = jnp.dot(h_rows.reshape(-1, model_width), w_qkv, preferred_element_type=jnp.float32).astype(jnp.bfloat16)
    packed = packed.reshape(blocks, length, 3, head_count, HD)
    queries = packed[:, :, 0].astype(jnp.float32)
    key_part = packed[:, :, 1].astype(jnp.float32)
    val_part = packed[:, :, 2].astype(jnp.float32)
    allowed = (region_codes[:, :, None] == region_codes[:, None, :])[:, None]
    scores = jnp.einsum('bqhe,bkhe->bhqk', queries, key_part) * score_scale
    scores = jnp.where(allowed, scores, -1e+30)
    highest = lax.optimization_barrier(jnp.max(scores, axis=-1, keepdims=True))
    exp_scores = jnp.exp(scores - highest)
    probs = exp_scores / lax.optimization_barrier(jnp.sum(exp_scores, axis=-1, keepdims=True))
    probs_low = probs.astype(jnp.bfloat16)
    head_mix = jnp.einsum('bhqk,bkhe->bqhe', probs_low.astype(jnp.float32), val_part).astype(jnp.bfloat16)
    head_mix = head_mix.reshape(blocks * length, model_width)
    attn_out = jnp.dot(head_mix, w_proj, preferred_element_type=jnp.float32).reshape(blocks, length, model_width)
    resid_mid = (wide_rows + attn_out).astype(jnp.bfloat16)
    normed_second, inv_second = row_stats(resid_mid.astype(jnp.float32))
    hidden_in = (normed_second * ln2_gain).astype(jnp.bfloat16).reshape(-1, model_width)
    preact = jnp.dot(hidden_in, w_fc1, preferred_element_type=jnp.float32) + b_fc1
    gelu_value, gelu_slope = gelu_pair(preact)
    hidden = gelu_value.astype(jnp.bfloat16)
    flat_up = up_rows.reshape(-1, model_width)
    grad_fc2 = jnp.dot(hidden.T, flat_up, preferred_element_type=jnp.float32)
    grad_pre = (jnp.dot(flat_up, w_fc2.T, preferred_element_type=jnp.float32) * gelu_slope).astype(jnp.bfloat16)
    grad_bias = lax.optimization_barrier(jnp.sum(grad_pre.astype(jnp.float32), axis=0))
    grad_fc1 = jnp.dot(hidden_in.T, grad_pre, preferred_element_type=jnp.float32)
    grad_norm = jnp.dot(grad_pre, w_fc1.T, preferred_element_type=jnp.float32).reshape(blocks, length, model_width)
    grad_mid, grad_gain2 = norm_back(grad_norm, normed_second, inv_second, ln2_gain)
    grad_res = up_rows.astype(jnp.float32) + grad_mid
    grad_attn = grad_res.astype(jnp.bfloat16).reshape(-1, model_width)
    grad_proj = jnp.dot(head_mix.T, grad_attn, preferred_element_type=jnp.float32)
    grad_mix = jnp.dot(grad_attn, w_proj.T, preferred_element_type=jnp.float32).astype(jnp.bfloat16)
    grad_mix = grad_mix.reshape(blocks, length, head_count, HD).astype(jnp.float32)
    grad_probs = jnp.einsum('bqhe,bkhe->bhqk', grad_mix, val_part)
    grad_val = jnp.einsum('bhqk,bqhe->bkhe', probs_low.astype(jnp.float32), grad_mix)
    grad_scores = probs * (grad_probs - lax.optimization_barrier(jnp.sum(probs * grad_probs, axis=-1, keepdims=True)))
    grad_low = (grad_scores * score_scale).astype(jnp.bfloat16).astype(jnp.float32)
    grad_query = jnp.einsum('bhqk,bkhe->bqhe', grad_low, key_part)
    grad_key = jnp.einsum('bhqk,bqhe->bkhe', grad_low, queries)
    grad_packed = jnp.stack((grad_query, grad_key, grad_val), axis=2).astype(jnp.bfloat16).reshape(-1, 3 * model_width)
    grad_qkv = jnp.dot(h_rows.reshape(-1, model_width).T, grad_packed, preferred_element_type=jnp.float32)
    grad_input = jnp.dot(grad_packed, w_qkv.T, preferred_element_type=jnp.float32).reshape(blocks, length, model_width)
    grad_tok, grad_gain1 = norm_back(grad_input, normed_first, inv_first, ln1_gain)
    result_rows = (grad_res + grad_tok).astype(jnp.bfloat16)
    return (result_rows, (grad_gain1, grad_qkv, grad_proj, grad_gain2, grad_fc1, grad_bias, grad_fc2))

def reference(tokens, upstream, window_labels, ln1_gain, w_qkv, w_proj, ln2_gain, w_fc1, b_fc1, w_fc2):
    shift_back = (WX // 2, WY // 2, WZ // 2)
    shift_ahead = (-(WX // 2), -(WY // 2), -(WZ // 2))
    moved_tok = jnp.roll(tokens, shift_ahead, axis=(0, 1, 2))
    moved_up = jnp.roll(upstream, shift_ahead, axis=(0, 1, 2))
    wrap_x = (jnp.arange(NX) >= NX - WX // 2).astype(jnp.int32)
    wrap_y = (jnp.arange(NY) >= NY - WY // 2).astype(jnp.int32)
    wrap_z = (jnp.arange(NZ) >= NZ - WZ // 2).astype(jnp.int32)
    code_grid = window_labels * 8 + wrap_x[:, None, None] * 4 + wrap_y[None, :, None] * 2 + wrap_z[None, None, :]
    tiles_x = NX // WX
    tiles_y = NY // WY

    def to_tiles(field_grid):
        trailing = field_grid.shape[3:]
        shaped = field_grid.reshape((tiles_x, WX, tiles_y, WY, NZ) + trailing)
        axes_order = (0, 2, 1, 3, 4) + tuple(range(5, 5 + len(trailing)))
        return shaped.transpose(axes_order).reshape((tiles_x * tiles_y, WX, WY, NZ) + trailing)
    zero_grads = (jnp.zeros((D,), jnp.float32), jnp.zeros((D, 3 * D), jnp.float32), jnp.zeros((D, D), jnp.float32), jnp.zeros((D,), jnp.float32), jnp.zeros((D, FF), jnp.float32), jnp.zeros((FF,), jnp.float32), jnp.zeros((FF, D), jnp.float32))

    def tile_step(carry, inputs):
        tok_tile, up_tile, code_tile = inputs
        wide_rows = to_windows(tok_tile, WZ).astype(jnp.float32)
        up_rows = to_windows(up_tile, WZ)
        region_codes = to_windows(code_tile, WZ)
        result_rows, grads = block_grads(wide_rows, up_rows, region_codes, ln1_gain, w_qkv, w_proj, ln2_gain, w_fc1, b_fc1, w_fc2)
        carry = tuple((left + right for left, right in zip(carry, grads)))
        return (carry, from_windows(result_rows, WX, WY, WZ))
    sums, result_tiles = lax.scan(tile_step, zero_grads, (to_tiles(moved_tok), to_tiles(moved_up), to_tiles(code_grid)))
    result_grid = result_tiles.reshape(tiles_x, tiles_y, WX, WY, NZ, D).transpose(0, 2, 1, 3, 4, 5).reshape(NX, NY, NZ, D)
    d_tokens = jnp.roll(result_grid, shift_back, axis=(0, 1, 2))
    param_total = 4 * D * D + 2 * D * FF + 2 * D + FF
    square_sum = jnp.zeros((), jnp.float32)
    for grad_term in sums:
        square_sum = square_sum + jnp.sum(grad_term * grad_term)
    factor = math.sqrt(param_total) * lax.rsqrt(square_sum)
    return (d_tokens, sums[0] * factor, (sums[1] * factor).astype(jnp.bfloat16), (sums[2] * factor).astype(jnp.bfloat16), sums[3] * factor, (sums[4] * factor).astype(jnp.bfloat16), sums[5] * factor, (sums[6] * factor).astype(jnp.bfloat16))
```

```python
import functools
import math

import jax
import jax.numpy as jnp
from jax import lax
from jax.experimental import pallas as pl
from jax.experimental.pallas import tpu as pltpu
from jax.sharding import PartitionSpec as P

HD = 32
WZ = 8
EPS = 1e-05
CUBIC = 0.044715
ROOT_TWO_PI = math.sqrt(2.0 / math.pi)
LOG2_E = 1.0 / math.log(2.0)
LANES = 128
PIECES = 32
BLOCKS = 4
EXTRA = 8
KERNEL_VMEM = 40 << 20
F32 = jnp.float32
BF16 = jnp.bfloat16


def dot(a, b):
    return jnp.dot(a, b, preferred_element_type=F32)


def dot_last(a, b):
    return lax.dot_general(a, b, (((1,), (1,)), ((), ())), preferred_element_type=F32)


def dot_first(a, b):
    return lax.dot_general(a, b, (((0,), (0,)), ((), ())), preferred_element_type=F32)


def row_stats(values):
    row_mean = jnp.mean(values, axis=-1, keepdims=True)
    center = values - row_mean
    variance = jnp.mean(center * center, axis=-1, keepdims=True)
    inv_std = lax.rsqrt(variance + EPS)
    return (center * inv_std, inv_std)


def norm_back(incoming, normed, inv_std, gain_vec):
    terms = incoming * normed
    scaled = incoming * gain_vec
    first_mean = jnp.mean(scaled, axis=-1, keepdims=True)
    second_mean = jnp.mean(terms * gain_vec, axis=-1, keepdims=True)
    back = inv_std * (scaled - first_mean - normed * second_mean)
    return (back, jnp.sum(terms, axis=0, keepdims=True))


def load_rows(part_refs):
    rows = [ref[...].astype(F32).reshape(-1, ref.shape[-1]) for ref in part_refs]
    return jnp.concatenate(rows, axis=0)


def head_columns(qkv, head, width):
    group, sub = divmod(head, LANES // HD)
    lo = group * LANES
    mine = lax.broadcasted_iota(jnp.int32, (1, LANES), 1) // HD == sub
    q, k, v = (qkv[:, i * width + lo : i * width + lo + LANES] for i in range(3))
    return (lo, sub, mine, q, k, v)


def put_block(stage, block, value, me):
    pieces = stage.shape[0] // BLOCKS
    rows = value.shape[0] // pieces
    for i in range(pieces):
        slot = (block * pieces + i) ^ me
        stage[slot, 0:rows] = value[i * rows : (i + 1) * rows]


def hand_out(stage, keep, send):
    half = stage.shape[0] // 2
    keep[...] = stage[:half]
    send[...] = stage[half:]


def forward_kernel(
    me, tok_a, tok_b, tok_c, tok_d, up_a, up_b, up_c, up_d, code_col, code_row,
    gain1, w_qkv, w_proj, gain2, w_fc1, b_fc1, w_fc2,
    keep_a, send_a, keep_b, send_b, small, grad_mid, normed1, inv1, qkv, probs, mix,
    allowed, stage_a, stage_b,
):
    width = w_proj.shape[0]
    heads = width // HD
    me_a, me_b = me[0], me[1]
    x = load_rows((tok_a, tok_b, tok_c, tok_d))
    normed, inv = row_stats(x)
    normed1[...] = normed
    inv1[...] = inv
    h1 = (normed * gain1[...]).astype(BF16)
    qkv[...] = dot(h1, w_qkv[...]).astype(BF16)
    allowed[...] = (code_col[...] == code_row[...]).astype(F32)

    for head in range(heads):
        lo, sub, mine, q, k, v = head_columns(qkv, head, width)
        scores = dot_last(jnp.where(mine, q, jnp.zeros_like(q)), k)
        scores = jnp.where(allowed[...] > 0.0, scores, -1e30)
        highest = jnp.max(scores, axis=-1, keepdims=True)
        weight = jnp.exp2((scores - highest) * (HD ** (-0.5) * LOG2_E))
        total = jnp.sum(weight, axis=-1, keepdims=True)
        prob = (weight * (1.0 / total)).astype(BF16)
        probs[head] = prob
        part = dot(prob, v)
        mix[:, lo : lo + LANES] = part if sub == 0 else jnp.where(mine, part, mix[:, lo : lo + LANES])

    mix_low = mix[...].astype(BF16)
    mid = (x + dot(mix_low, w_proj[...])).astype(BF16).astype(F32)
    normed2, inv2 = row_stats(mid)
    h2 = (normed2 * gain2[...]).astype(BF16)
    up = load_rows((up_a, up_b, up_c, up_d))
    up_low = up.astype(BF16)

    t2 = None
    for j in range(BLOCKS):
        cols = slice(j * width, (j + 1) * width)
        pre = dot(h2, w_fc1[:, cols]) + b_fc1[:, cols]
        square = pre * pre
        tanh_value = jnp.tanh(ROOT_TWO_PI * pre * (1.0 + CUBIC * square))
        half = 0.5 * (1.0 + tanh_value)
        hidden = (pre * half).astype(BF16)
        slope = half + 0.5 * pre * (1.0 - tanh_value * tanh_value) * (
            ROOT_TWO_PI * (1.0 + 3.0 * CUBIC * square)
        )
        put_block(stage_a, j, dot_first(hidden, up_low).astype(BF16), me_a)
        gp = (dot_last(up_low, w_fc2[cols, :]) * slope).astype(BF16)
        small[1 + j : 2 + j, :] = jnp.sum(gp.astype(F32), axis=0, keepdims=True)
        put_block(stage_b, j, dot_first(h2, gp).astype(BF16), me_b)
        part = dot_last(gp, w_fc1[:, cols])
        t2 = part if t2 is None else t2 + part
    back2, s_ln2 = norm_back(t2, normed2, inv2, gain2[...])
    small[0:1, :] = s_ln2
    grad_mid[...] = up + back2
    hand_out(stage_a, keep_a, send_a)
    hand_out(stage_b, keep_b, send_b)


def backward_kernel(
    me, small, grad_mid, normed1, inv1, qkv, probs, mix, gain1, w_qkv, w_proj,
    out_a, out_b, out_c, out_d, keep_t, send_t,
    dmix, dqkv, stage_t,
):
    width = w_proj.shape[0]
    heads = width // HD
    score_scale = HD ** (-0.5)
    me_t = me[0]
    grad_attn = grad_mid[...].astype(BF16)
    dmix[...] = dot_last(grad_attn, w_proj[...]).astype(BF16)
    pieces, rows, _ = stage_t.shape
    stage_t[:, rows - EXTRA :] = jnp.zeros((pieces, EXTRA, width), BF16)
    for i in range(BLOCKS + 1):
        slot = (i + 1) ^ me_t
        stage_t[slot, rows - EXTRA : rows - EXTRA + 1] = small[i : i + 1, :].astype(BF16)
    put_block(stage_t, 3, dot_first(mix[...].astype(BF16), grad_attn).astype(BF16), me_t)

    for head in range(heads):
        lo, sub, mine, q, k, v = head_columns(qkv, head, width)
        do = dmix[:, lo : lo + LANES]
        do_mine = jnp.where(mine, do, jnp.zeros_like(do))
        delta = jnp.sum(do_mine.astype(F32) * mix[:, lo : lo + LANES], axis=-1, keepdims=True)
        prob = probs[head]
        ds = (prob.astype(F32) * (dot_last(do_mine, v) - delta)).astype(BF16)
        parts = (dot(ds, k) * score_scale, dot_first(ds, q) * score_scale, dot_first(prob, do))
        for i, part in enumerate(parts):
            at = i * width + lo
            dqkv[:, at : at + LANES] = (
                part if sub == 0 else jnp.where(mine, part, dqkv[:, at : at + LANES])
            )

    dqkv_low = dqkv[...].astype(BF16)
    normed = normed1[...]
    h1 = (normed * gain1[...]).astype(BF16)
    t1 = None
    for j in range(3):
        cols = slice(j * width, (j + 1) * width)
        put_block(stage_t, j, dot_first(h1, dqkv_low[:, cols]).astype(BF16), me_t)
        part = dot_last(dqkv_low[:, cols], w_qkv[:, cols])
        t1 = part if t1 is None else t1 + part
    back1, s_ln1 = norm_back(t1, normed, inv1[...], gain1[...])
    stage_t[me_t, rows - EXTRA : rows - EXTRA + 1] = s_ln1.astype(BF16)
    hand_out(stage_t, keep_t, send_t)
    result = grad_mid[...] + back1
    quarter = result.shape[0] // 4
    for i, ref in enumerate((out_a, out_b, out_c, out_d)):
        ref[...] = result[i * quarter : (i + 1) * quarter].reshape(ref.shape).astype(BF16)


def finish_kernel(*refs):
    (me, stats), refs = refs[:2], refs[2:]
    parts, (g_qkv, g_proj, g_fc1, g_fc2, g_small, both) = refs[:-6], refs[-6:]
    each = len(parts) // 3
    width = g_proj.shape[0]
    pieces = PIECES // BLOCKS
    total = jnp.sum(stats[...], keepdims=True)
    factor = jnp.sqrt(float(param_count(width, g_fc1.shape[1]))) * lax.rsqrt(total)
    g_small[...] = jnp.zeros_like(g_small)
    for kind in range(3):
        for i, ref in enumerate(parts[kind * each : (kind + 1) * each]):
            for j in range(ref.shape[0]):
                piece = (i * ref.shape[0] + j) ^ me[kind]
                value = ref[j].astype(F32) * factor
                rows = width // pieces
                block, row = piece // pieces, pl.multiple_of(piece % pieces * rows, rows)
                low = value[:rows].astype(BF16)
                if kind == 0:
                    g_fc2[pl.ds(pl.multiple_of(piece * rows, rows), rows), :] = low
                else:
                    into = g_fc1 if kind == 1 else both
                    into[pl.ds(row, rows), pl.ds(pl.multiple_of(block * width, width), width)] = low
                if kind == 2:
                    g_small[piece] = value[rows:]
    g_qkv[...] = both[:, : 3 * width]
    g_proj[...] = both[:, 3 * width :]


def param_count(width, ff):
    return 4 * width * width + 2 * width * ff + 2 * width + ff


VMEM = pl.BlockSpec(memory_space=pltpu.VMEM)
SMEM = pl.BlockSpec(memory_space=pltpu.SMEM)


def shape(dims, dtype):
    return jax.ShapeDtypeStruct(dims, dtype)


def call(kernel, outs, scratch, flops, *args):
    moved = sum(a.size * a.dtype.itemsize for a in args) + sum(
        math.prod(o.shape) * o.dtype.itemsize for o in outs
    )
    return pl.pallas_call(
        kernel,
        out_shape=outs,
        in_specs=[SMEM] + [VMEM] * (len(args) - 1),
        out_specs=(VMEM,) * len(outs),
        scratch_shapes=scratch,
        cost_estimate=pl.CostEstimate(flops=flops, bytes_accessed=moved, transcendentals=0),
        compiler_params=pltpu.CompilerParams(vmem_limit_bytes=KERNEL_VMEM),
    )(*args)


def neighbour(shard, step_x, step_y):
    size_x, size_y = lax.axis_size("gx"), lax.axis_size("gy")
    pairs = [
        (x * size_y + y, (x + step_x) % size_x * size_y + (y + step_y) % size_y)
        for x in range(size_x)
        for y in range(size_y)
    ]
    return lax.ppermute(shard, ("gx", "gy"), pairs)


def quarters(tile):
    half_x, half_y = tile.shape[0] // 2, tile.shape[1] // 2
    return (
        tile[half_x:, half_y:],
        neighbour(tile[half_x:, :half_y], 0, -1),
        neighbour(tile[:half_x, half_y:], -1, 0),
        neighbour(tile[:half_x, :half_y], -1, -1),
    )


def window_codes(labels):
    tile_x, tile_y, tile_z = labels.shape
    half_x, half_y = tile_x // 2, tile_y // 2
    last_x = (lax.axis_index("gx") == lax.axis_size("gx") - 1).astype(jnp.int32)
    last_y = (lax.axis_index("gy") == lax.axis_size("gy") - 1).astype(jnp.int32)
    upper_x = (jnp.arange(tile_x) >= half_x).astype(jnp.int32)
    upper_y = (jnp.arange(tile_y) >= half_y).astype(jnp.int32)
    upper_z = (jnp.arange(tile_z) >= tile_z - WZ // 2).astype(jnp.int32)
    codes = (
        labels * 8
        + (4 * last_x) * upper_x[:, None, None]
        + (2 * last_y) * upper_y[None, :, None]
        + upper_z[None, None, :]
    )
    codes = jnp.roll(codes, WZ // 2, axis=2)
    parts = (
        codes[:half_x, :half_y], codes[:half_x, half_y:],
        codes[half_x:, :half_y], codes[half_x:, half_y:],
    )
    return jnp.concatenate([part.reshape(-1) for part in parts])


def swap(shard, flip_x, flip_y):
    size_x, size_y = lax.axis_size("gx"), lax.axis_size("gy")
    pairs = [
        (x * size_y + y, (x ^ flip_x) * size_y + (y ^ flip_y))
        for x in range(size_x)
        for y in range(size_y)
    ]
    return lax.ppermute(shard, ("gx", "gy"), pairs)


def add(first, *others):
    total = first.astype(F32)
    for other in others:
        total = total + other.astype(F32)
    return total


CORE, SIDE = (0, 1), (0, 2)
NEAR, FAR = (1, 0), ((2, 0), (4, 0), (6, 0))
ORDERS = ((CORE, SIDE, NEAR), (CORE, NEAR, SIDE), (CORE, SIDE, NEAR))


def place(order):
    index_x, index_y = lax.axis_index("gx"), lax.axis_index("gy")
    number = jnp.int32(0)
    for flip_x, flip_y in order:
        bit = (index_x & flip_x) if flip_x else (index_y & flip_y)
        number = 2 * number + (bit != 0).astype(jnp.int32)
    return 4 * number + ((index_x // 2) & 3)


def scatter_sum(keep, send, order):
    for step, flips in enumerate(order):
        got = swap(send, *flips)
        if step == len(order) - 1:
            break
        half = keep.shape[0] // 2
        keep, send = (
            add(keep[:half], got[:half]).astype(BF16),
            add(keep[half:], got[half:]).astype(BF16),
        )
    last = [add(keep[i], got[i]) for i in range(keep.shape[0])]
    own = add(last[0], *(swap(last[i + 1].astype(BF16), *flips) for i, flips in enumerate(FAR)))
    for axis, spare in (("gx", 8), ("gy", 4)):
        while spare < lax.axis_size(axis):
            flips = (spare, 0) if axis == "gx" else (0, spare)
            own = add(own.astype(BF16), swap(own.astype(BF16), *flips))
            spare *= 2
    return own


def gather(own, order):
    parts = [jnp.stack([own] + [swap(own, *flips) for flips in FAR])]
    for flips in reversed(order):
        parts = parts + [swap(part, *flips) for part in parts]
    return parts


def body(tokens, upstream, window_labels, ln1_gain, w_qkv, w_proj, ln2_gain, w_fc1, b_fc1, w_fc2):
    width, ff = w_fc1.shape
    heads = width // HD
    tok_parts = quarters(tokens)
    up_parts = quarters(upstream)
    codes = window_codes(window_labels)
    rows = codes.shape[0]
    me = jnp.stack([place(order) for order in ORDERS])
    piece = BLOCKS * width // PIECES
    half = shape((PIECES // 2, piece, width), BF16)
    half_t = shape((PIECES // 2, piece + EXTRA, width), BF16)
    gain1 = ln1_gain[None, :]
    outs = call(
        forward_kernel,
        (half, half, half, half)
        + (shape((1 + BLOCKS, width), F32), shape((rows, width), F32), shape((rows, width), F32), shape((rows, 1), F32))
        + (shape((rows, 3 * width), BF16), shape((heads, rows, rows), BF16), shape((rows, width), F32)),
        [
            pltpu.VMEM((rows, rows), F32),
            pltpu.VMEM((PIECES, piece, width), BF16),
            pltpu.VMEM((PIECES, piece, width), BF16),
        ],
        2 * rows * width * (4 * width + 5 * ff) + 4 * heads * rows * rows * LANES,
        me, *tok_parts, *up_parts, codes[:, None], codes[None, :],
        gain1, w_qkv, w_proj, ln2_gain[None, :], w_fc1, b_fc1[None, :], w_fc2,
    )
    keep_a, send_a, keep_b, send_b = outs[:4]
    sum_a = scatter_sum(keep_a, send_a, ORDERS[0])
    sum_b = scatter_sum(keep_b, send_b, ORDERS[1])
    done = call(
        backward_kernel,
        (shape(tok_parts[0].shape, BF16),) * 4 + (half_t, half_t),
        [
            pltpu.VMEM((rows, width), BF16),
            pltpu.VMEM((rows, 3 * width), F32),
            pltpu.VMEM((PIECES, piece + EXTRA, width), BF16),
        ],
        2 * rows * width * 8 * width + 8 * heads * rows * rows * LANES,
        me[2:], *outs[4:], gain1, w_qkv, w_proj,
    )
    sum_t = scatter_sum(done[4], done[5], ORDERS[2])
    square = jnp.sum(sum_a * sum_a) + jnp.sum(sum_b * sum_b) + jnp.sum(sum_t * sum_t)
    high = square.astype(BF16)
    lower = square - high.astype(F32)
    middle = lower.astype(BF16)
    at = lax.broadcasted_iota(jnp.int32, sum_t.shape, 0) - piece
    own_t = jnp.where(at == 1, high, jnp.where(at == 2, middle, sum_t.astype(BF16)))
    parts_a = gather(sum_a.astype(BF16), ORDERS[0])
    parts_b = gather(sum_b.astype(BF16), ORDERS[1])
    parts_t = gather(own_t, ORDERS[2])
    stats = jnp.concatenate([part[:, piece + 1 : piece + 3, 0] for part in parts_t]).astype(F32)
    g_qkv, g_proj, g_fc1, g_fc2, g_small = call(
        finish_kernel,
        (
            shape((width, 3 * width), BF16), shape((width, width), BF16),
            shape((width, ff), BF16), shape((ff, width), BF16), shape((PIECES, EXTRA, width), F32),
        ),
        [pltpu.VMEM((width, 4 * width), BF16)],
        4 * width * width,
        me, stats, *parts_a, *parts_b, *parts_t,
    )
    back = (done[0], neighbour(done[1], 0, 1), neighbour(done[2], 1, 0), neighbour(done[3], 1, 1))
    result = jnp.concatenate(
        (
            jnp.concatenate((back[3], back[2]), axis=1),
            jnp.concatenate((back[1], back[0]), axis=1),
        ),
        axis=0,
    )
    return (
        result, g_small[0, 0], g_qkv, g_proj, g_small[1, 0], g_fc1,
        g_small[2 : 2 + BLOCKS, 0].reshape(ff), g_fc2,
    )


def solution(mesh):
    return jax.shard_map(
        body,
        mesh=mesh,
        in_specs=(
            P("gx", "gy", None, None),
            P("gx", "gy", None, None),
            P("gx", "gy", None),
            P(), P(), P(), P(), P(), P(), P(),
        ),
        out_specs=(P("gx", "gy", None, None), P(), P(), P(), P(), P(), P(), P()),
        check_vma=False,
    )
```

```python
import functools
import math

import jax
import jax.numpy as jnp
from jax import lax
from jax.experimental import pallas as pl
from jax.experimental.pallas import tpu as pltpu
from jax.sharding import PartitionSpec as P

HD = 32
WZ = 8
EPS = 1e-05
CUBIC = 0.044715
ROOT_TWO_PI = math.sqrt(2.0 / math.pi)
LOG2_E = 1.0 / math.log(2.0)
LANES = 128
PIECES = 16
BLOCKS = 4
EXTRA = 8
EARLY = 2
KERNEL_VMEM = 40 << 20
F32 = jnp.float32
BF16 = jnp.bfloat16


def dot(a, b):
    return jnp.dot(a, b, preferred_element_type=F32)


def dot_last(a, b):
    return lax.dot_general(a, b, (((1,), (1,)), ((), ())), preferred_element_type=F32)


def dot_first(a, b):
    return lax.dot_general(a, b, (((0,), (0,)), ((), ())), preferred_element_type=F32)


def row_stats(values):
    row_mean = jnp.mean(values, axis=-1, keepdims=True)
    center = values - row_mean
    variance = jnp.mean(center * center, axis=-1, keepdims=True)
    inv_std = lax.rsqrt(variance + EPS)
    return (center * inv_std, inv_std)


def norm_back(incoming, normed, inv_std, gain_vec):
    terms = incoming * normed
    scaled = incoming * gain_vec
    first_mean = jnp.mean(scaled, axis=-1, keepdims=True)
    second_mean = jnp.mean(terms * gain_vec, axis=-1, keepdims=True)
    back = inv_std * (scaled - first_mean - normed * second_mean)
    return (back, jnp.sum(terms, axis=0, keepdims=True))


def head_columns(qkv, head, width):
    group, sub = divmod(head, LANES // HD)
    lo = group * LANES
    mine = lax.broadcasted_iota(jnp.int32, (1, LANES), 1) // HD == sub
    q, k, v = (qkv[:, i * width + lo : i * width + lo + LANES] for i in range(3))
    return (lo, sub, mine, q, k, v)


def low_slot(piece, me, order):
    half = PIECES // 2
    return (piece % half) ^ me[1 + 2 * order + piece // half]


def put_block(stage, block, value, me, order, top=0):
    pieces = PIECES // BLOCKS
    rows = value.shape[0] // pieces
    for i in range(pieces):
        piece = block * pieces + i
        core = piece // (PIECES // 2)
        slot = (core ^ me[0]) * (PIECES // 2) + low_slot(piece, me, order)
        stage[slot, top : top + rows] = value[i * rows : (i + 1) * rows]


def hand_out(stage, keep, send):
    half = stage.shape[0] // 2
    keep[...] = stage[:half]
    send[...] = stage[half:]


def load_window(own, parts, index):
    half_x, half_y = own.shape[0] // 2, own.shape[1] // 2
    rows = [own[half_x:, half_y:]] + [part[index] for part in parts]
    return jnp.concatenate([r.astype(F32).reshape(-1, r.shape[-1]) for r in rows], axis=0)


def forward_kernel(
    me, tok, up_own, part_b, part_c, part_d, code_col, code_row,
    gain1, gain2, b_fc1, w_qkv, w_proj_far, w_fc1_far, w_fc2_far,
    keep, send, small, grad_mid, normed1, inv1, qkv, probs, mix,
    allowed, stage, w_proj, w_fc1, w_fc2, sems,
):
    far = (w_proj_far, w_fc2_far, w_fc1_far)
    near = (w_proj, w_fc2, w_fc1)
    fetch = [pltpu.make_async_copy(a, b, sems.at[i]) for i, (a, b) in enumerate(zip(far, near))]
    for copy in fetch:
        copy.start()
    width = w_proj.shape[0]
    heads = width // HD
    piece = stage.shape[1] // 2
    parts = (part_b, part_c, part_d)
    x = load_window(tok, parts, 0)
    normed, inv = row_stats(x)
    normed1[...] = normed
    inv1[...] = inv
    h1 = (normed * gain1[...]).astype(BF16)
    qkv[...] = dot(h1, w_qkv[...]).astype(BF16)
    allowed[...] = (code_col[...] == code_row[...]).astype(F32)

    for head in range(heads):
        lo, sub, mine, q, k, v = head_columns(qkv, head, width)
        scores = dot_last(jnp.where(mine, q, jnp.zeros_like(q)), k)
        scores = jnp.where(allowed[...] > 0.0, scores, -1e30)
        highest = jnp.max(scores, axis=-1, keepdims=True)
        weight = jnp.exp2((scores - highest) * (HD ** (-0.5) * LOG2_E))
        total = jnp.sum(weight, axis=-1, keepdims=True)
        prob = (weight * (1.0 / total)).astype(BF16)
        probs[head] = prob
        part = dot(prob, v)
        mix[:, lo : lo + LANES] = part if sub == 0 else jnp.where(mine, part, mix[:, lo : lo + LANES])

    for copy in fetch:
        copy.wait()
    mix_low = mix[...].astype(BF16)
    mid = (x + dot(mix_low, w_proj[...])).astype(BF16).astype(F32)
    normed2, inv2 = row_stats(mid)
    h2 = (normed2 * gain2[...]).astype(BF16)
    up = load_window(up_own, parts, 1)
    up_low = up.astype(BF16)

    t2 = None
    for j in range(BLOCKS):
        cols = slice(j * width, (j + 1) * width)
        pre = dot(h2, w_fc1[:, cols]) + b_fc1[:, cols]
        square = pre * pre
        tanh_value = jnp.tanh(ROOT_TWO_PI * pre * (1.0 + CUBIC * square))
        half = 0.5 * (1.0 + tanh_value)
        hidden = (pre * half).astype(BF16)
        slope = half + 0.5 * pre * (1.0 - tanh_value * tanh_value) * (
            ROOT_TWO_PI * (1.0 + 3.0 * CUBIC * square)
        )
        put_block(stage, j, dot_first(hidden, up_low).astype(BF16), me, 0)
        gp = (dot_last(up_low, w_fc2[cols, :]) * slope).astype(BF16)
        small[1 + j : 2 + j, :] = jnp.sum(gp.astype(F32), axis=0, keepdims=True)
        put_block(stage, j, dot_first(h2, gp).astype(BF16), me, 0, piece)
        part = dot_last(gp, w_fc1[:, cols])
        t2 = part if t2 is None else t2 + part
    back2, s_ln2 = norm_back(t2, normed2, inv2, gain2[...])
    small[0:1, :] = s_ln2
    grad_mid[...] = up + back2
    hand_out(stage, keep, send)


def heads_back(groups, qkv, probs, mix, dmix, dqkv):
    width = mix.shape[1]
    score_scale = HD ** (-0.5)
    per_group = LANES // HD
    for group in groups:
        sums = None
        for head in range(group * per_group, (group + 1) * per_group):
            lo, sub, mine, q, k, v = head_columns(qkv, head, width)
            do = dmix[:, lo : lo + LANES]
            do_mine = jnp.where(mine, do, jnp.zeros_like(do))
            delta = jnp.sum(do_mine.astype(F32) * mix[:, lo : lo + LANES], axis=-1, keepdims=True)
            prob = probs[head]
            ds = (prob.astype(F32) * (dot_last(do_mine, v) - delta)).astype(BF16)
            parts = (dot(ds, k) * score_scale, dot_first(ds, q) * score_scale, dot_first(prob, do))
            sums = parts if sums is None else [jnp.where(mine, a, b) for a, b in zip(parts, sums)]
        for i, part in enumerate(sums):
            dqkv[:, i * width + lo : i * width + lo + LANES] = part.astype(BF16)


def first_back_kernel(me, grad_mid, qkv, probs, mix, w_proj, dmix, dqkv):
    dmix[...] = dot_last(grad_mid[...].astype(BF16), w_proj[...]).astype(BF16)
    heads_back(range(EARLY), qkv, probs, mix, dmix, dqkv)


def second_back_kernel(
    me, small, grad_mid, normed1, inv1, qkv, probs, mix, dmix, dqkv_early, gain1, w_qkv,
    out_a, out_b, out_c, out_d, keep_t, send_t,
    dqkv, stage_t,
):
    width = mix.shape[1]
    pieces, rows, _ = stage_t.shape
    stage_t[:, rows - EXTRA :] = jnp.zeros((pieces, EXTRA, width), BF16)
    extra = [me[0] * (PIECES // 2) + low_slot(i, me, 1) for i in range(BLOCKS + 2)]
    for i in range(BLOCKS + 1):
        stage_t[extra[i + 1], rows - EXTRA : rows - EXTRA + 1] = small[i : i + 1, :].astype(BF16)
    grad_attn = grad_mid[...].astype(BF16)
    put_block(stage_t, 3, dot_first(mix[...].astype(BF16), grad_attn).astype(BF16), me, 1)
    heads_back(range(EARLY, width // LANES), qkv, probs, mix, dmix, dqkv)
    normed = normed1[...]
    h1 = (normed * gain1[...]).astype(BF16)
    t1 = None
    early = EARLY * LANES
    for j in range(3):
        lo = j * width
        own = jnp.concatenate(
            [dqkv_early[:, lo : lo + early], dqkv[:, lo + early : lo + width]], axis=1
        )
        put_block(stage_t, j, dot_first(h1, own).astype(BF16), me, 1)
        part = dot_last(own, w_qkv[:, lo : lo + width])
        t1 = part if t1 is None else t1 + part
    back1, s_ln1 = norm_back(t1, normed, inv1[...], gain1[...])
    stage_t[extra[0], rows - EXTRA : rows - EXTRA + 1] = s_ln1.astype(BF16)
    hand_out(stage_t, keep_t, send_t)
    result = grad_mid[...] + back1
    quarter = result.shape[0] // 4
    for i, ref in enumerate((out_a, out_b, out_c, out_d)):
        ref[...] = result[i * quarter : (i + 1) * quarter].reshape(ref.shape).astype(BF16)


def finish_kernel(*refs):
    me, back_a, back_b, back_c, back_d = refs[:5]
    parts = refs[5:-14]
    out, g_ln1, g_qkv, g_proj, g_ln2, g_fc1, g_bfc1, g_fc2 = refs[-14:-6]
    out_near, fc1, fc2, both, smalls, sems = refs[-6:]
    half = PIECES // 2
    width, ff = fc1.shape
    rows = width * BLOCKS // PIECES
    half_x, half_y = out_near.shape[0] // 2, out_near.shape[1] // 2
    copies = []

    def leave(source, target):
        copies.append(pltpu.make_async_copy(source, target, sems.at[len(copies)]))
        copies[-1].start()

    out_near[half_x:, half_y:] = back_a[...]
    out_near[half_x:, :half_y] = back_b[...]
    out_near[:half_x, half_y:] = back_c[...]
    out_near[:half_x, :half_y] = back_d[...]
    leave(out_near, out)
    total = jnp.zeros((8, width), F32)
    for ref in parts:
        for j in range(ref.shape[0]):
            value = ref[j].astype(F32)
            total = total + jnp.sum((value * value).reshape(-1, 8, width), axis=0)
    total = jnp.sum(jnp.sum(total, axis=0, keepdims=True), axis=1, keepdims=True)
    factor = math.sqrt(param_count(width, ff)) * lax.rsqrt(total)
    per_block = PIECES // BLOCKS
    slots_t = [arrivals(ORDERS[1], core) for core in range(2)]

    def spot(core, order, slot):
        piece = core * half + (slot ^ jnp.where(core == 0, me[1 + 2 * order], me[2 + 2 * order]))
        top = pl.multiple_of(piece % per_block * rows, rows)
        left = pl.multiple_of(piece // per_block * width, width)
        return piece, pl.ds(top, rows), pl.ds(left, width)

    for kind in range(2):
        for i, ref in enumerate(parts):
            core = me[0] ^ (i // 2)
            for j in range(ref.shape[0]):
                slot = i % 2 * ref.shape[0] + j
                if kind == 0:
                    value = ref[j, : 2 * rows].astype(F32) * factor
                    piece, down, across = spot(core, 0, slot)
                    fc2[pl.ds(pl.multiple_of(piece * rows, rows), rows), :] = value[:rows].astype(BF16)
                    fc1[down, across] = value[rows:].astype(BF16)
                else:
                    value = ref[j, 2 * rows :].astype(F32) * factor
                    slot_t = jnp.where(core == 0, slots_t[0][slot], slots_t[1][slot])
                    piece, down, across = spot(core, 1, slot_t)
                    both[down, across] = value[:rows].astype(BF16)
                    smalls[piece] = value[rows:]
        if kind == 0:
            leave(fc2, g_fc2)
            leave(fc1, g_fc1)
        else:
            leave(both.at[:, : 3 * width], g_qkv)
            leave(both.at[:, 3 * width :], g_proj)
    g_ln1[...] = smalls[0, 0]
    g_ln2[...] = smalls[1, 0]
    for j in range(BLOCKS):
        g_bfc1[j * width : (j + 1) * width] = smalls[2 + j, 0]
    for copy in copies:
        copy.wait()


def param_count(width, ff):
    return 4 * width * width + 2 * width * ff + 2 * width + ff


VMEM = pl.BlockSpec(memory_space=pltpu.VMEM)
SMEM = pl.BlockSpec(memory_space=pltpu.SMEM)
HBM = pl.BlockSpec(memory_space=pltpu.HBM)


def shape(dims, dtype):
    return jax.ShapeDtypeStruct(dims, dtype)


def like(*arrays):
    return [pltpu.VMEM(a.shape, a.dtype) for a in arrays]


def call(kernel, outs, scratch, flops, me, near, far=(), out_specs=None):
    far = tuple(pltpu.with_memory_space_constraint(a, pltpu.HBM) for a in far)
    args = (me, *near, *far)
    moved = sum(a.size * a.dtype.itemsize for a in args) + sum(
        math.prod(o.shape) * o.dtype.itemsize for o in outs
    )
    return pl.pallas_call(
        kernel,
        out_shape=outs,
        in_specs=[SMEM] + [VMEM] * len(near) + [HBM] * len(far),
        out_specs=out_specs or (VMEM,) * len(outs),
        scratch_shapes=scratch,
        cost_estimate=pl.CostEstimate(flops=flops, bytes_accessed=moved, transcendentals=0),
        compiler_params=pltpu.CompilerParams(vmem_limit_bytes=KERNEL_VMEM),
    )(*args)


def neighbour(shard, step_x, step_y):
    size_x, size_y = lax.axis_size("gx"), lax.axis_size("gy")
    pairs = [
        (x * size_y + y, (x + step_x) % size_x * size_y + (y + step_y) % size_y)
        for x in range(size_x)
        for y in range(size_y)
    ]
    return lax.ppermute(shard, ("gx", "gy"), pairs)


def arriving(tile):
    half_x, half_y = tile.shape[1] // 2, tile.shape[2] // 2
    return (
        neighbour(tile[:, half_x:, :half_y], 0, -1),
        neighbour(tile[:, :half_x, half_y:], -1, 0),
        neighbour(tile[:, :half_x, :half_y], -1, -1),
    )


def window_codes(labels):
    tile_x, tile_y, tile_z = labels.shape
    half_x, half_y = tile_x // 2, tile_y // 2
    last_x = (lax.axis_index("gx") == lax.axis_size("gx") - 1).astype(jnp.int32)
    last_y = (lax.axis_index("gy") == lax.axis_size("gy") - 1).astype(jnp.int32)
    upper_x = (jnp.arange(tile_x) >= half_x).astype(jnp.int32)
    upper_y = (jnp.arange(tile_y) >= half_y).astype(jnp.int32)
    upper_z = (jnp.arange(tile_z) >= tile_z - WZ // 2).astype(jnp.int32)
    codes = (
        labels * 8
        + (4 * last_x) * upper_x[:, None, None]
        + (2 * last_y) * upper_y[None, :, None]
        + upper_z[None, None, :]
    )
    codes = jnp.roll(codes, WZ // 2, axis=2)
    parts = (
        codes[:half_x, :half_y], codes[:half_x, half_y:],
        codes[half_x:, :half_y], codes[half_x:, half_y:],
    )
    return jnp.concatenate([part.reshape(-1) for part in parts])


def swap(shard, flips):
    size_x, size_y = lax.axis_size("gx"), lax.axis_size("gy")
    pairs = [
        (x * size_y + y, (x ^ flips[y % 2][0]) * size_y + (y ^ flips[y % 2][1]))
        for x in range(size_x)
        for y in range(size_y)
    ]
    return lax.ppermute(shard, ("gx", "gy"), pairs)


def add(first, *others):
    total = first.astype(F32)
    for other in others:
        total = total + other.astype(F32)
    return total


SIDE, NEAR, LAYER = (0, 2), (1, 0), (2, 0)
CORE = ((0, 1), (0, 1))
SPARE = 4
ORDERS = (
    ((SIDE, LAYER), (NEAR, SIDE), (LAYER, NEAR)),
    ((NEAR, NEAR), (LAYER, LAYER), (SIDE, SIDE)),
)


def arrivals(order, core):
    slots = [0]
    for flips in reversed(ORDERS[0]):
        bit = 2 - [step[core] for step in order].index(flips[core])
        slots = slots + [slot | 1 << bit for slot in slots]
    return slots


def place():
    index_x, index_y = lax.axis_index("gx"), lax.axis_index("gy")
    numbers = [index_y % 2]
    for order in ORDERS:
        for core in range(2):
            number = jnp.int32(0)
            for flips in order:
                flip_x, flip_y = flips[core]
                bit = (index_x & flip_x) if flip_x else (index_y & flip_y)
                number = 2 * number + (bit != 0).astype(jnp.int32)
            numbers.append(number)
    return jnp.stack(numbers)


def fold(keep, got):
    half = keep.shape[0] // 2
    return (
        add(keep[:half], got[:half]).astype(BF16),
        add(keep[half:], got[half:]).astype(BF16),
    )


def after(values, first):
    return lax.optimization_barrier((*values, first))[: len(values)]


def spares():
    for axis in (0, 1):
        spare = SPARE
        while spare < lax.axis_size(("gx", "gy")[axis]):
            yield ((spare, 0) if axis == 0 else (0, spare),) * 2
            spare *= 2


def reduce_all(keep, send, got, keep_t, send_t, away):
    order, order_t = ORDERS
    got_t, = after([swap(send_t, CORE)], send)
    keep_t, send_t = fold(keep_t, got_t)
    for step in range(3):
        got_t = swap(send_t, order_t[step])
        got, = after([got], send_t)
        if step < 2:
            keep, send = fold(keep, got)
            got = swap(send, order[step + 1])
            got_t, = after([got_t], send)
            keep_t, send_t = fold(keep_t, got_t)
        else:
            low = add(keep[0], got[0]).astype(BF16)
            got_t, = after([got_t], low)
            low_t = add(keep_t[0], got_t[0]).astype(BF16)
    for flips in spares():
        got, got_t = swap(low, flips), swap(low_t, flips)
        low = add(low, after([got], low_t)[0]).astype(BF16)
        low_t = add(low_t, after([got_t], low)[0]).astype(BF16)
    own = jnp.concatenate([low, low_t])[None]
    two = jnp.concatenate([own, swap(own, order[2])])
    four = jnp.concatenate([two, swap(two, order[1])])
    side = swap(four, order[0])
    away = after(away, four)
    back = [neighbour(away[0], 0, 1), neighbour(away[1], 1, 0), neighbour(away[2], 1, 1)]
    side, *back = after([side, *back], four)
    return back, [four, side, swap(four, CORE), swap(side, CORE)]


def body(tokens, upstream, window_labels, ln1_gain, w_qkv, w_proj, ln2_gain, w_fc1, b_fc1, w_fc2):
    width, ff = w_fc1.shape
    heads = width // HD
    parts = arriving(jnp.stack([tokens, upstream]))
    codes = window_codes(window_labels)
    rows = codes.shape[0]
    me = place()
    piece = BLOCKS * width // PIECES
    half = shape((PIECES // 2, 2 * piece, width), BF16)
    half_t = shape((PIECES // 2, piece + EXTRA, width), BF16)
    gain1 = ln1_gain[None, :]
    keep, send, *saved = call(
        forward_kernel,
        (half, half)
        + (shape((1 + BLOCKS, width), F32), shape((rows, width), F32), shape((rows, width), F32), shape((rows, 1), F32))
        + (shape((rows, 3 * width), BF16), shape((heads, rows, rows), BF16), shape((rows, width), F32)),
        [pltpu.VMEM((rows, rows), F32), pltpu.VMEM((PIECES, 2 * piece, width), BF16)]
        + like(w_proj, w_fc1, w_fc2)
        + [pltpu.SemaphoreType.DMA((3,))],
        2 * rows * width * (4 * width + 5 * ff) + 4 * heads * rows * rows * LANES,
        me,
        (tokens, upstream, *parts, codes[:, None], codes[None, :], gain1, ln2_gain[None, :], b_fc1[None, :], w_qkv),
        (w_proj, w_fc1, w_fc2),
    )
    quarter = shape(parts[0].shape[1:], BF16)
    small, grad_mid, normed1, inv1, qkv, probs, mix = saved
    got = swap(send, CORE)
    dmix, dqkv = call(
        first_back_kernel,
        (shape((rows, width), BF16), shape((rows, 3 * width), BF16)),
        [],
        2 * rows * width * width + 8 * EARLY * (LANES // HD) * rows * rows * LANES,
        me,
        (grad_mid, qkv, probs, mix, w_proj),
    )
    got, = after([got], dmix)
    keep, send = fold(keep, got)
    got = swap(send, ORDERS[0][0])
    dmix, = after([dmix], send)
    *done, keep_t, send_t = call(
        second_back_kernel,
        (quarter,) * 4 + (half_t, half_t),
        [pltpu.VMEM((rows, 3 * width), BF16), pltpu.VMEM((PIECES, piece + EXTRA, width), BF16)],
        2 * rows * width * 7 * width + 8 * (heads - EARLY * (LANES // HD)) * rows * rows * LANES,
        me,
        (small, grad_mid, normed1, inv1, qkv, probs, mix, dmix, dqkv, gain1, w_qkv),
    )
    back, slots = reduce_all(keep, send, got, keep_t, send_t, done[1:])
    result, g_ln1, g_qkv, g_proj, g_ln2, g_fc1, g_bfc1, g_fc2 = call(
        finish_kernel,
        (
            shape(tokens.shape, BF16), shape((width,), F32), shape((width, 3 * width), BF16),
            shape((width, width), BF16), shape((width,), F32), shape((width, ff), BF16),
            shape((ff,), F32), shape((ff, width), BF16),
        ),
        like(tokens, w_fc1, w_fc2)
        + [
            pltpu.VMEM((width, 4 * width), BF16),
            pltpu.VMEM((PIECES, EXTRA, width), F32),
            pltpu.SemaphoreType.DMA((5,)),
        ],
        4 * width * width,
        me,
        (done[0], *back, *slots),
        out_specs=(HBM, VMEM, HBM, HBM, VMEM, HBM, VMEM, HBM),
    )
    return (result, g_ln1, g_qkv, g_proj, g_ln2, g_fc1, g_bfc1, g_fc2)


def solution(mesh):
    return jax.shard_map(
        body,
        mesh=mesh,
        in_specs=(
            P("gx", "gy", None, None),
            P("gx", "gy", None, None),
            P("gx", "gy", None),
            P(), P(), P(), P(), P(), P(), P(),
        ),
        out_specs=(P("gx", "gy", None, None), P(), P(), P(), P(), P(), P(), P()),
        check_vma=False,
    )
```

```python
import functools
import math

import jax
import jax.numpy as jnp
from jax import lax
from jax.experimental import pallas as pl
from jax.experimental.pallas import tpu as pltpu
from jax.sharding import PartitionSpec as P

HD = 32
WZ = 8
EPS = 1e-05
CUBIC = 0.044715
ROOT_TWO_PI = math.sqrt(2.0 / math.pi)
LOG2_E = 1.0 / math.log(2.0)
LANES = 128
PIECES = 16
BLOCKS = 4
EXTRA = 8
EARLY = 2
KERNEL_VMEM = 40 << 20
F32 = jnp.float32
BF16 = jnp.bfloat16


def dot(a, b):
    return jnp.dot(a, b, preferred_element_type=F32)


def dot_last(a, b):
    return lax.dot_general(a, b, (((1,), (1,)), ((), ())), preferred_element_type=F32)


def dot_first(a, b):
    return lax.dot_general(a, b, (((0,), (0,)), ((), ())), preferred_element_type=F32)


def row_stats(values):
    row_mean = jnp.mean(values, axis=-1, keepdims=True)
    center = values - row_mean
    variance = jnp.mean(center * center, axis=-1, keepdims=True)
    inv_std = lax.rsqrt(variance + EPS)
    return (center * inv_std, inv_std)


def norm_back(incoming, normed, inv_std, gain_vec):
    terms = incoming * normed
    scaled = incoming * gain_vec
    first_mean = jnp.mean(scaled, axis=-1, keepdims=True)
    second_mean = jnp.mean(terms * gain_vec, axis=-1, keepdims=True)
    back = inv_std * (scaled - first_mean - normed * second_mean)
    return (back, jnp.sum(terms, axis=0, keepdims=True))


def head_columns(qkv, head, width):
    group, sub = divmod(head, LANES // HD)
    lo = group * LANES
    mine = lax.broadcasted_iota(jnp.int32, (1, LANES), 1) // HD == sub
    q, k, v = (qkv[:, i * width + lo : i * width + lo + LANES] for i in range(3))
    return (lo, sub, mine, q, k, v)


def low_slot(piece, me, order):
    half = PIECES // 2
    return (piece % half) ^ me[1 + 2 * order + piece // half]


def put_block(stage, value, me, order, top, first=0, pieces=PIECES):
    rows = value.shape[0] // pieces
    for i in range(pieces):
        piece = first + i
        core = piece // (PIECES // 2)
        slot = (core ^ me[0]) * (PIECES // 2) + low_slot(piece, me, order)
        stage[slot, top : top + rows] = value[i * rows : (i + 1) * rows]


def hand_out(stage, keep, send):
    half = stage.shape[0] // 2
    keep[...] = stage[:half]
    send[...] = stage[half:]


def load_window(own, parts, index):
    half_x, half_y = own.shape[0] // 2, own.shape[1] // 2
    rows = [own[half_x:, half_y:]] + [part[index] for part in parts]
    return jnp.concatenate([r.astype(F32).reshape(-1, r.shape[-1]) for r in rows], axis=0)


def fetch_kernel(*refs):
    count = (len(refs) - 2) // 2
    copies = [
        pltpu.make_async_copy(refs[1 + i], refs[1 + count + i], refs[-1].at[i]) for i in range(count)
    ]
    for copy in copies:
        copy.start()
    for copy in copies:
        copy.wait()


def forward_kernel(
    me, tok, up_own, part_b, part_c, part_d, code_col, code_row,
    gain1, gain2, b_fc1, w_qkv, w_proj, w_fc1_far, w_fc2_far,
    keep, send, small, grad_mid, normed1, inv1, qkv, probs, mix,
    allowed, stage, pre_all, up_hidden, hidden_all, grad_pre, w_fc1, w_fc2, sems,
):
    fetch = [
        pltpu.make_async_copy(w_fc1_far, w_fc1, sems.at[0]),
        pltpu.make_async_copy(w_fc2_far, w_fc2, sems.at[1]),
    ]
    for copy in fetch:
        copy.start()
    width = w_proj.shape[0]
    heads = width // HD
    each = PIECES // BLOCKS
    piece = each * width * BLOCKS // (PIECES * each)
    parts = (part_b, part_c, part_d)
    x = load_window(tok, parts, 0)
    normed, inv = row_stats(x)
    normed1[...] = normed
    inv1[...] = inv
    h1 = (normed * gain1[...][None, :]).astype(BF16)
    qkv[...] = dot(h1, w_qkv[...]).astype(BF16)
    allowed[...] = (code_col[...] == code_row[...]).astype(F32)

    for head in range(heads):
        lo, sub, mine, q, k, v = head_columns(qkv, head, width)
        scores = dot_last(jnp.where(mine, q, jnp.zeros_like(q)), k)
        scores = jnp.where(allowed[...] > 0.0, scores, -1e30)
        highest = jnp.max(scores, axis=-1, keepdims=True)
        weight = jnp.exp2((scores - highest) * (HD ** (-0.5) * LOG2_E))
        total = jnp.sum(weight, axis=-1, keepdims=True)
        prob = (weight * (1.0 / total)).astype(BF16)
        probs[head] = prob
        part = dot(prob, v)
        mix[:, lo : lo + LANES] = part if sub == 0 else jnp.where(mine, part, mix[:, lo : lo + LANES])

    for copy in fetch:
        copy.wait()
    mix_low = mix[...].astype(BF16)
    mid = (x + dot(mix_low, w_proj[...])).astype(BF16).astype(F32)
    normed2, inv2 = row_stats(mid)
    h2 = (normed2 * gain2[...][None, :]).astype(BF16)
    up = load_window(up_own, parts, 1)
    up_low = up.astype(BF16)

    pre_all[...] = dot(h2, w_fc1[...])
    up_hidden[...] = dot_last(up_low, w_fc2[...])
    count = pre_all.shape[0]
    chunk = 32
    bias = b_fc1[...][None, :]
    total = None
    for i in range(count // chunk):
        at = slice(i * chunk, (i + 1) * chunk)
        pre = pre_all[at, :] + bias
        square = pre * pre
        tanh_value = jnp.tanh(pre * (ROOT_TWO_PI + (ROOT_TWO_PI * CUBIC) * square))
        half = 0.5 + 0.5 * tanh_value
        hidden_all[at, :] = (pre * half).astype(BF16)
        slope = half + pre * (1.0 - tanh_value * tanh_value) * (
            0.5 * ROOT_TWO_PI + (1.5 * ROOT_TWO_PI * CUBIC) * square
        )
        gp = (up_hidden[at, :] * slope).astype(BF16)
        grad_pre[at, :] = gp
        part = jnp.sum(gp.astype(F32).reshape(chunk // 8, 8, -1), axis=0)
        total = part if total is None else total + part
    total = jnp.sum(total, axis=0, keepdims=True)
    for j in range(BLOCKS):
        small[1 + j : 2 + j, :] = total[:, j * width : (j + 1) * width]
    put_block(stage, dot_first(hidden_all[...], up_low).astype(BF16), me, 0, 0)
    t2 = dot_last(grad_pre[...], w_fc1[...])
    grad = dot_first(h2, grad_pre[...]).astype(BF16)
    for j in range(BLOCKS):
        put_block(stage, grad[:, j * width : (j + 1) * width], me, 0, piece, j * each, each)
    back2, s_ln2 = norm_back(t2, normed2, inv2, gain2[...][None, :])
    small[0:1, :] = s_ln2
    grad_res = up + back2
    grad_mid[...] = grad_res
    grad_proj = dot_first(mix_low, grad_res.astype(BF16)).astype(BF16)
    put_block(stage, grad_proj, me, 0, 2 * piece)
    hand_out(stage, keep, send)


def heads_back(groups, qkv, probs, mix, dmix, dqkv):
    width = mix.shape[1]
    score_scale = HD ** (-0.5)
    per_group = LANES // HD
    for group in groups:
        sums = None
        for head in range(group * per_group, (group + 1) * per_group):
            lo, sub, mine, q, k, v = head_columns(qkv, head, width)
            do = dmix[:, lo : lo + LANES]
            do_mine = jnp.where(mine, do, jnp.zeros_like(do))
            delta = jnp.sum(do_mine.astype(F32) * mix[:, lo : lo + LANES], axis=-1, keepdims=True)
            prob = probs[head]
            ds = (prob.astype(F32) * (dot_last(do_mine, v) - delta)).astype(BF16)
            parts = (dot(ds, k) * score_scale, dot_first(ds, q) * score_scale, dot_first(prob, do))
            sums = parts if sums is None else [jnp.where(mine, a, b) for a, b in zip(parts, sums)]
        for i, part in enumerate(sums):
            dqkv[:, i * width + lo : i * width + lo + LANES] = part.astype(BF16)


def first_back_kernel(me, grad_mid, qkv, probs, mix, w_proj, dmix, dqkv):
    dmix[...] = dot_last(grad_mid[...].astype(BF16), w_proj[...]).astype(BF16)
    heads_back(range(EARLY), qkv, probs, mix, dmix, dqkv)


def second_back_kernel(
    me, small, grad_mid, normed1, inv1, qkv, probs, mix, dmix, dqkv_early, gain1, w_qkv,
    out_a, out_b, out_c, out_d, keep_t, send_t,
    dqkv, stage_t,
):
    width = mix.shape[1]
    pieces, rows, _ = stage_t.shape
    stage_t[:, rows - EXTRA :] = jnp.zeros((pieces, EXTRA, width), BF16)
    extra = [me[0] * (PIECES // 2) + low_slot(i, me, 1) for i in range(BLOCKS + 2)]
    for i in range(BLOCKS + 1):
        stage_t[extra[i + 1], rows - EXTRA : rows - EXTRA + 1] = small[i : i + 1, :].astype(BF16)
    heads_back(range(EARLY, width // LANES), qkv, probs, mix, dmix, dqkv)
    normed = normed1[...]
    h1 = (normed * gain1[...][None, :]).astype(BF16)
    early = EARLY * LANES
    for j in range(3):
        lo = j * width
        dqkv[:, lo : lo + early] = dqkv_early[:, lo : lo + early]
    grad = dot_first(h1, dqkv[...]).astype(BF16)
    for j in range(3):
        put_block(stage_t, grad[:, j * width : (j + 1) * width], me, 1, j * width // PIECES)
    t1 = dot_last(dqkv[...], w_qkv[...])
    back1, s_ln1 = norm_back(t1, normed, inv1[...], gain1[...][None, :])
    stage_t[extra[0], rows - EXTRA : rows - EXTRA + 1] = s_ln1.astype(BF16)
    hand_out(stage_t, keep_t, send_t)
    result = grad_mid[...] + back1
    quarter = result.shape[0] // 4
    for i, ref in enumerate((out_a, out_b, out_c, out_d)):
        ref[...] = result[i * quarter : (i + 1) * quarter].reshape(ref.shape).astype(BF16)


def finish_kernel(*refs):
    me, back_a, back_b, back_c, back_d = refs[:5]
    parts = refs[5:-15]
    out, g_ln1, g_qkv, g_proj, g_ln2, g_fc1, g_bfc1, g_fc2 = refs[-15:-7]
    out_near, fc1, fc2, qkv, proj, smalls, sems = refs[-7:]
    half = PIECES // 2
    width, ff = fc1.shape
    rows = width * BLOCKS // PIECES
    thin = width // PIECES
    half_x, half_y = out_near.shape[0] // 2, out_near.shape[1] // 2
    copies = []

    def leave(source, target):
        copies.append(pltpu.make_async_copy(source, target, sems.at[len(copies)]))
        copies[-1].start()

    out_near[half_x:, half_y:] = back_a[...]
    out_near[half_x:, :half_y] = back_b[...]
    out_near[:half_x, half_y:] = back_c[...]
    out_near[:half_x, :half_y] = back_d[...]
    leave(out_near, out)
    total = jnp.zeros((8, width), F32)
    for ref in parts:
        for j in range(ref.shape[0]):
            value = ref[j].astype(F32)
            total = total + jnp.sum((value * value).reshape(-1, 8, width), axis=0)
    total = jnp.sum(jnp.sum(total, axis=0, keepdims=True), axis=1, keepdims=True)
    factor = math.sqrt(param_count(width, ff)) * lax.rsqrt(total)
    per_block = PIECES // BLOCKS
    def spot(core, order, slot):
        piece = core * half + (slot ^ jnp.where(core == 0, me[1 + 2 * order], me[2 + 2 * order]))
        top = pl.multiple_of(piece % per_block * rows, rows)
        left = pl.multiple_of(piece // per_block * width, width)
        return piece, pl.ds(top, rows), pl.ds(left, width)

    for kind in range(2):
        for i, ref in enumerate(parts[4 * kind : 4 * kind + 4]):
            core = me[0] ^ (i // 2)
            for j in range(ref.shape[0]):
                slot = i % 2 * ref.shape[0] + j
                if kind == 0:
                    value = (ref[j].astype(F32) * factor).astype(BF16)
                    piece, down, across = spot(core, 0, slot)
                    fc2[pl.ds(pl.multiple_of(piece * rows, rows), rows), :] = value[:rows]
                    fc1[down, across] = value[rows : 2 * rows]
                    proj[piece] = value[2 * rows :]
                else:
                    value = ref[j].astype(F32) * factor
                    piece, down, across = spot(core, 1, slot)
                    for part in range(3):
                        at = slice(part * width, (part + 1) * width)
                        qkv[piece, :, at] = value[part * thin : (part + 1) * thin].astype(BF16)
                    smalls[piece] = value[3 * thin :]
        if kind == 0:
            leave(fc2, g_fc2)
            leave(fc1, g_fc1)
            leave(proj, g_proj)
        else:
            leave(qkv, g_qkv)
    g_ln1[...] = smalls[0, 0]
    g_ln2[...] = smalls[1, 0]
    for j in range(BLOCKS):
        g_bfc1[j * width : (j + 1) * width] = smalls[2 + j, 0]
    for copy in copies:
        copy.wait()


def param_count(width, ff):
    return 4 * width * width + 2 * width * ff + 2 * width + ff


VMEM = pl.BlockSpec(memory_space=pltpu.VMEM)
SMEM = pl.BlockSpec(memory_space=pltpu.SMEM)
HBM = pl.BlockSpec(memory_space=pltpu.HBM)


def shape(dims, dtype):
    return jax.ShapeDtypeStruct(dims, dtype)


def like(*arrays):
    return [pltpu.VMEM(a.shape, a.dtype) for a in arrays]


def call(kernel, outs, scratch, flops, me, near, far=(), out_specs=None):
    far = tuple(pltpu.with_memory_space_constraint(a, pltpu.HBM) for a in far)
    args = (me, *near, *far)
    moved = sum(a.size * a.dtype.itemsize for a in args) + sum(
        math.prod(o.shape) * o.dtype.itemsize for o in outs
    )
    return pl.pallas_call(
        kernel,
        out_shape=outs,
        in_specs=[SMEM] + [VMEM] * len(near) + [HBM] * len(far),
        out_specs=out_specs or (VMEM,) * len(outs),
        scratch_shapes=scratch,
        cost_estimate=pl.CostEstimate(flops=flops, bytes_accessed=moved, transcendentals=0),
        compiler_params=pltpu.CompilerParams(vmem_limit_bytes=KERNEL_VMEM),
    )(*args)


def neighbour(shard, step_x, step_y):
    size_x, size_y = lax.axis_size("gx"), lax.axis_size("gy")
    pairs = [
        (x * size_y + y, (x + step_x) % size_x * size_y + (y + step_y) % size_y)
        for x in range(size_x)
        for y in range(size_y)
    ]
    return lax.ppermute(shard, ("gx", "gy"), pairs)


def arriving(tile):
    half_x, half_y = tile.shape[1] // 2, tile.shape[2] // 2
    return (
        neighbour(tile[:, half_x:, :half_y], 0, -1),
        neighbour(tile[:, :half_x, half_y:], -1, 0),
        neighbour(tile[:, :half_x, :half_y], -1, -1),
    )


def window_codes(labels):
    tile_x, tile_y, tile_z = labels.shape
    half_x, half_y = tile_x // 2, tile_y // 2
    last_x = (lax.axis_index("gx") == lax.axis_size("gx") - 1).astype(jnp.int32)
    last_y = (lax.axis_index("gy") == lax.axis_size("gy") - 1).astype(jnp.int32)
    upper_x = (jnp.arange(tile_x) >= half_x).astype(jnp.int32)
    upper_y = (jnp.arange(tile_y) >= half_y).astype(jnp.int32)
    upper_z = (jnp.arange(tile_z) >= tile_z - WZ // 2).astype(jnp.int32)
    codes = (
        labels * 8
        + (4 * last_x) * upper_x[:, None, None]
        + (2 * last_y) * upper_y[None, :, None]
        + upper_z[None, None, :]
    )
    codes = jnp.roll(codes, WZ // 2, axis=2)
    parts = (
        codes[:half_x, :half_y], codes[:half_x, half_y:],
        codes[half_x:, :half_y], codes[half_x:, half_y:],
    )
    return jnp.concatenate([part.reshape(-1) for part in parts])


def swap(shard, flips):
    size_x, size_y = lax.axis_size("gx"), lax.axis_size("gy")
    pairs = [
        (x * size_y + y, (x ^ flips[y % 2][0]) * size_y + (y ^ flips[y % 2][1]))
        for x in range(size_x)
        for y in range(size_y)
    ]
    return lax.ppermute(shard, ("gx", "gy"), pairs)


def add(first, *others):
    total = first.astype(F32)
    for other in others:
        total = total + other.astype(F32)
    return total


SIDE, NEAR, LAYER = (0, 2), (1, 0), (2, 0)
CORE = ((0, 1), (0, 1))
SPARE = 4
ORDERS = (
    ((SIDE, LAYER), (NEAR, SIDE), (LAYER, NEAR)),
    ((NEAR, NEAR), (LAYER, LAYER), (SIDE, SIDE)),
)


def place():
    index_x, index_y = lax.axis_index("gx"), lax.axis_index("gy")
    numbers = [index_y % 2]
    for order in ORDERS:
        for core in range(2):
            number = jnp.int32(0)
            for flips in order:
                flip_x, flip_y = flips[core]
                bit = (index_x & flip_x) if flip_x else (index_y & flip_y)
                number = 2 * number + (bit != 0).astype(jnp.int32)
            numbers.append(number)
    return jnp.stack(numbers)


def fold(keep, got):
    half = keep.shape[0] // 2
    return (
        add(keep[:half], got[:half]).astype(BF16),
        add(keep[half:], got[half:]).astype(BF16),
    )


def after(values, first):
    return lax.optimization_barrier((*values, first))[: len(values)]


def spares():
    for axis in (0, 1):
        spare = SPARE
        while spare < lax.axis_size(("gx", "gy")[axis]):
            yield ((spare, 0) if axis == 0 else (0, spare),) * 2
            spare *= 2


def reduce_all(keep, send, got, keep_t, send_t, away):
    order, order_t = ORDERS
    got_t, = after([swap(send_t, CORE)], send)
    keep_t, send_t = fold(keep_t, got_t)
    for step in range(3):
        got_t = swap(send_t, order_t[step])
        got, = after([got], send_t)
        if step < 2:
            keep, send = fold(keep, got)
            got = swap(send, order[step + 1])
            got_t, = after([got_t], send)
            keep_t, send_t = fold(keep_t, got_t)
        else:
            low = add(keep[0], got[0]).astype(BF16)
            got_t, = after([got_t], low)
            low_t = add(keep_t[0], got_t[0]).astype(BF16)
    for flips in spares():
        got, got_t = swap(low, flips), swap(low_t, flips)
        low = add(low, after([got], low_t)[0]).astype(BF16)
        low_t = add(low_t, after([got_t], low)[0]).astype(BF16)
    parts, parts_t = low[None], low_t[None]
    for step in (2, 1, 0):
        more, more_t = swap(parts, order[step]), swap(parts_t, order_t[step])
        if step == 0:
            away = after(away, parts)
            back = [neighbour(away[0], 0, 1), neighbour(away[1], 1, 0), neighbour(away[2], 1, 1)]
            more, more_t, *back = lax.optimization_barrier((more, more_t, *back))
            break
        more, more_t = lax.optimization_barrier((more, more_t))
        parts, parts_t = jnp.concatenate([parts, more]), jnp.concatenate([parts_t, more_t])
    streams = ((parts, more), (parts_t, more_t))
    return back, [part for pair in streams for part in (*pair, swap(pair[0], CORE), swap(pair[1], CORE))]


def body(tokens, upstream, window_labels, ln1_gain, w_qkv, w_proj, ln2_gain, w_fc1, b_fc1, w_fc2):
    width, ff = w_fc1.shape
    heads = width // HD
    parts = arriving(jnp.stack([tokens, upstream]))
    codes = window_codes(window_labels)
    rows = codes.shape[0]
    me = place()
    piece = BLOCKS * width // PIECES
    thin = width // PIECES
    rows_f, rows_t = 2 * piece + thin, 3 * thin + EXTRA
    half = shape((PIECES // 2, rows_f, width), BF16)
    half_t = shape((PIECES // 2, rows_t, width), BF16)
    weights = (w_qkv, w_proj)
    weights = call(
        fetch_kernel, tuple(shape(w.shape, BF16) for w in weights), [pltpu.SemaphoreType.DMA((2,))], 0, me, (), weights
    )
    w_qkv, w_proj = weights
    parts = after(parts, w_proj)
    keep, send, *saved = call(
        forward_kernel,
        (half, half)
        + (shape((1 + BLOCKS, width), F32), shape((rows, width), F32), shape((rows, width), F32), shape((rows, 1), F32))
        + (shape((rows, 3 * width), BF16), shape((heads, rows, rows), BF16), shape((rows, width), F32)),
        [pltpu.VMEM((rows, rows), F32), pltpu.VMEM((PIECES, rows_f, width), BF16), pltpu.VMEM((rows, ff), F32), pltpu.VMEM((rows, ff), F32), pltpu.VMEM((rows, ff), BF16), pltpu.VMEM((rows, ff), BF16)]
        + like(w_fc1, w_fc2)
        + [pltpu.SemaphoreType.DMA((2,))],
        2 * rows * width * (4 * width + 5 * ff) + 4 * heads * rows * rows * LANES,
        me,
        (tokens, upstream, *parts, codes[:, None], codes[None, :], ln1_gain, ln2_gain, b_fc1, w_qkv, w_proj),
        (w_fc1, w_fc2),
    )
    quarter = shape(parts[0].shape[1:], BF16)
    small, grad_mid, normed1, inv1, qkv, probs, mix = saved
    got = swap(send, CORE)
    dmix, dqkv = call(
        first_back_kernel,
        (shape((rows, width), BF16), shape((rows, 3 * width), BF16)),
        [],
        2 * rows * width * width + 8 * EARLY * (LANES // HD) * rows * rows * LANES,
        me,
        (grad_mid, qkv, probs, mix, w_proj),
    )
    got, = after([got], dmix)
    keep, send = fold(keep, got)
    got = swap(send, ORDERS[0][0])
    dmix, = after([dmix], send)
    *done, keep_t, send_t = call(
        second_back_kernel,
        (quarter,) * 4 + (half_t, half_t),
        [pltpu.VMEM((rows, 3 * width), BF16), pltpu.VMEM((PIECES, rows_t, width), BF16)],
        2 * rows * width * 7 * width + 8 * (heads - EARLY * (LANES // HD)) * rows * rows * LANES,
        me,
        (small, grad_mid, normed1, inv1, qkv, probs, mix, dmix, dqkv, ln1_gain, w_qkv),
    )
    back, slots = reduce_all(keep, send, got, keep_t, send_t, done[1:])
    result, g_ln1, g_qkv, g_proj, g_ln2, g_fc1, g_bfc1, g_fc2 = call(
        finish_kernel,
        (
            shape(tokens.shape, BF16), shape((width,), F32), shape((PIECES, thin, 3 * width), BF16),
            shape((PIECES, thin, width), BF16), shape((width,), F32), shape((width, ff), BF16),
            shape((ff,), F32), shape((ff, width), BF16),
        ),
        like(tokens, w_fc1, w_fc2)
        + [
            pltpu.VMEM((PIECES, thin, 3 * width), BF16),
            pltpu.VMEM((PIECES, thin, width), BF16),
            pltpu.VMEM((PIECES, EXTRA, width), F32),
            pltpu.SemaphoreType.DMA((5,)),
        ],
        4 * width * width,
        me,
        (done[0], *back, *slots),
        out_specs=(HBM, VMEM, HBM, HBM, VMEM, HBM, VMEM, HBM),
    )
    g_qkv, g_proj = g_qkv.reshape(width, 3 * width), g_proj.reshape(width, width)
    return (result, g_ln1, g_qkv, g_proj, g_ln2, g_fc1, g_bfc1, g_fc2)


def solution(mesh):
    return jax.shard_map(
        body,
        mesh=mesh,
        in_specs=(
            P("gx", "gy", None, None),
            P("gx", "gy", None, None),
            P("gx", "gy", None),
            P(), P(), P(), P(), P(), P(), P(),
        ),
        out_specs=(P("gx", "gy", None, None), P(), P(), P(), P(), P(), P(), P()),
        check_vma=False,
    )
```

```python
import functools
import math

import jax
import jax.numpy as jnp
from jax import lax
from jax.experimental import pallas as pl
from jax.experimental.pallas import tpu as pltpu
from jax.sharding import PartitionSpec as P

HD = 32
WZ = 8
EPS = 1e-05
CUBIC = 0.044715
ROOT_TWO_PI = math.sqrt(2.0 / math.pi)
LOG2_E = 1.0 / math.log(2.0)
LANES = 128
PIECES = 16
BLOCKS = 4
EXTRA = 8
KERNEL_VMEM = 40 << 20
F32 = jnp.float32
BF16 = jnp.bfloat16


def dot(a, b):
    return jnp.dot(a, b, preferred_element_type=F32)


def dot_last(a, b):
    return lax.dot_general(a, b, (((1,), (1,)), ((), ())), preferred_element_type=F32)


def dot_first(a, b):
    return lax.dot_general(a, b, (((0,), (0,)), ((), ())), preferred_element_type=F32)


def row_stats(values):
    row_mean = jnp.mean(values, axis=-1, keepdims=True)
    center = values - row_mean
    variance = jnp.mean(center * center, axis=-1, keepdims=True)
    inv_std = lax.rsqrt(variance + EPS)
    return (center * inv_std, inv_std)


def norm_back(incoming, normed, inv_std, gain_vec):
    terms = incoming * normed
    scaled = incoming * gain_vec
    first_mean = jnp.mean(scaled, axis=-1, keepdims=True)
    second_mean = jnp.mean(terms * gain_vec, axis=-1, keepdims=True)
    back = inv_std * (scaled - first_mean - normed * second_mean)
    return (back, jnp.sum(terms, axis=0, keepdims=True))


def head_columns(qkv, head, width):
    group, sub = divmod(head, LANES // HD)
    lo = group * LANES
    mine = lax.broadcasted_iota(jnp.int32, (1, LANES), 1) // HD == sub
    q, k, v = (qkv[:, i * width + lo : i * width + lo + LANES] for i in range(3))
    return (lo, sub, mine, q, k, v)


def low_slot(piece, me, order):
    half = PIECES // 2
    return (piece % half) ^ me[1 + 2 * order + piece // half]


def put_block(stage, value, me, order, top, first=0, pieces=PIECES):
    rows = value.shape[0] // pieces
    for i in range(pieces):
        piece = first + i
        core = piece // (PIECES // 2)
        slot = (core ^ me[0]) * (PIECES // 2) + low_slot(piece, me, order)
        stage[slot, top : top + rows] = value[i * rows : (i + 1) * rows]


def hand_out(stage, keep, send):
    half = stage.shape[0] // 2
    keep[...] = stage[:half]
    send[...] = stage[half:]


def load_window(own, parts, index):
    half_x, half_y = own.shape[0] // 2, own.shape[1] // 2
    rows = [own[half_x:, half_y:]] + [part[index] for part in parts]
    return jnp.concatenate([r.astype(F32).reshape(-1, r.shape[-1]) for r in rows], axis=0)


def fetch_kernel(*refs):
    count = (len(refs) - 2) // 2
    copies = [
        pltpu.make_async_copy(refs[1 + i], refs[1 + count + i], refs[-1].at[i]) for i in range(count)
    ]
    for copy in copies:
        copy.start()
    for copy in copies:
        copy.wait()


def forward_kernel(
    me, tok, up_own, part_b, part_c, part_d, code_col, code_row,
    gain1, gain2, b_fc1, w_qkv, w_proj, w_fc1_far, w_fc2_far,
    keep, send, small, grad_mid, normed1, inv1, qkv, probs, mix,
    allowed, stage, pre_all, up_hidden, hidden_all, grad_pre, w_fc1, w_fc2, sems,
):
    fetch = [
        pltpu.make_async_copy(w_fc1_far, w_fc1, sems.at[0]),
        pltpu.make_async_copy(w_fc2_far, w_fc2, sems.at[1]),
    ]
    for copy in fetch:
        copy.start()
    width = w_proj.shape[0]
    heads = width // HD
    rows = allowed.shape[0]
    each = PIECES // BLOCKS
    piece = each * width * BLOCKS // (PIECES * each)
    parts = (part_b, part_c, part_d)
    x = load_window(tok, parts, 0)
    normed, inv = row_stats(x)
    normed1[...] = normed
    inv1[...] = inv
    h1 = (normed * gain1[...][None, :]).astype(BF16)
    qkv[...] = dot(h1, w_qkv[...]).astype(BF16)
    allowed[...] = (code_col[...] == code_row[...]).astype(F32)

    together = 4
    for first in range(0, heads, together):
        masks = []
        for head in range(first, first + together):
            lo, sub, mine, q, k, v = head_columns(qkv, head, width)
            masks.append(mine)
        stacked = jnp.concatenate([jnp.where(mine, q, jnp.zeros_like(q)) for mine in masks], axis=0)
        scores = dot_last(stacked, k).reshape(together, rows, rows)
        scores = jnp.where(allowed[...][None] > 0.0, scores, -1e30)
        highest = jnp.max(scores, axis=-1, keepdims=True)
        weight = jnp.exp2((scores - highest) * (HD ** (-0.5) * LOG2_E))
        total = jnp.sum(weight, axis=-1, keepdims=True)
        prob = (weight * (1.0 / total)).astype(BF16)
        probs[first : first + together] = prob
        part = dot(prob.reshape(together * rows, rows), v).reshape(together, rows, LANES)
        for i, mine in enumerate(masks):
            old = mix[:, lo : lo + LANES] if (first + i) % (LANES // HD) else None
            mix[:, lo : lo + LANES] = part[i] if old is None else jnp.where(mine, part[i], old)

    for copy in fetch:
        copy.wait()
    mix_low = mix[...].astype(BF16)
    mid = (x + dot(mix_low, w_proj[...])).astype(BF16).astype(F32)
    normed2, inv2 = row_stats(mid)
    h2 = (normed2 * gain2[...][None, :]).astype(BF16)
    up = load_window(up_own, parts, 1)
    up_low = up.astype(BF16)

    pre_all[...] = dot(h2, w_fc1[...])
    up_hidden[...] = dot_last(up_low, w_fc2[...])
    count = pre_all.shape[0]
    chunk = 32
    bias = b_fc1[...][None, :]
    total = None
    for i in range(count // chunk):
        at = slice(i * chunk, (i + 1) * chunk)
        pre = pre_all[at, :] + bias
        square = pre * pre
        tanh_value = jnp.tanh(pre * (ROOT_TWO_PI + (ROOT_TWO_PI * CUBIC) * square))
        half = 0.5 + 0.5 * tanh_value
        hidden_all[at, :] = (pre * half).astype(BF16)
        slope = half + pre * (1.0 - tanh_value * tanh_value) * (
            0.5 * ROOT_TWO_PI + (1.5 * ROOT_TWO_PI * CUBIC) * square
        )
        gp = (up_hidden[at, :] * slope).astype(BF16)
        grad_pre[at, :] = gp
        part = jnp.sum(gp.astype(F32).reshape(chunk // 8, 8, -1), axis=0)
        total = part if total is None else total + part
    total = jnp.sum(total, axis=0, keepdims=True)
    for j in range(BLOCKS):
        small[1 + j : 2 + j, :] = total[:, j * width : (j + 1) * width]
    put_block(stage, dot_first(hidden_all[...], up_low).astype(BF16), me, 0, 0)
    t2 = dot_last(grad_pre[...], w_fc1[...])
    grad = dot_first(h2, grad_pre[...]).astype(BF16)
    for j in range(BLOCKS):
        put_block(stage, grad[:, j * width : (j + 1) * width], me, 0, piece, j * each, each)
    back2, s_ln2 = norm_back(t2, normed2, inv2, gain2[...][None, :])
    small[0:1, :] = s_ln2
    grad_mid[...] = up + back2
    hand_out(stage, keep, send)


def heads_back(qkv, probs, mix, dmix, dqkv):
    width = mix.shape[1]
    score_scale = HD ** (-0.5)
    per_group = LANES // HD
    for group in range(width // LANES):
        sums = None
        together = 4
        for first in range(group * per_group, (group + 1) * per_group, together):
            masks, deltas, dos = [], [], []
            for head in range(first, first + together):
                lo, sub, mine, q, k, v = head_columns(qkv, head, width)
                do = dmix[:, lo : lo + LANES]
                do_mine = jnp.where(mine, do, jnp.zeros_like(do))
                deltas.append(jnp.sum(do_mine.astype(F32) * mix[:, lo : lo + LANES], axis=-1, keepdims=True))
                masks.append(mine)
                dos.append(do_mine)
            rows = do.shape[0]
            prob = probs[first : first + together]
            dp = dot_last(jnp.concatenate(dos, axis=0), v).reshape(together, rows, rows)
            ds = (prob.astype(F32) * (dp - jnp.stack(deltas))).astype(BF16)
            dq = dot(ds.reshape(together * rows, rows), k).reshape(together, rows, LANES)
            for i, mine in enumerate(masks):
                parts = (dq[i] * score_scale, dot_first(ds[i], q) * score_scale, dot_first(prob[i], do))
                sums = parts if sums is None else [jnp.where(mine, a, b) for a, b in zip(parts, sums)]
        for i, part in enumerate(sums):
            dqkv[:, i * width + lo : i * width + lo + LANES] = part.astype(BF16)


def backward_kernel(
    me, small, grad_mid, normed1, inv1, qkv, probs, mix, gain1, w_qkv, w_proj,
    out_a, out_b, out_c, out_d, keep_t, send_t,
    dmix, dqkv, stage_t,
):
    width = mix.shape[1]
    pieces, rows, _ = stage_t.shape
    stage_t[:, rows - EXTRA :] = jnp.zeros((pieces, EXTRA, width), BF16)
    extra = [me[0] * (PIECES // 2) + low_slot(i, me, 1) for i in range(BLOCKS + 2)]
    for i in range(BLOCKS + 1):
        stage_t[extra[i + 1], rows - EXTRA : rows - EXTRA + 1] = small[i : i + 1, :].astype(BF16)
    grad_attn = grad_mid[...].astype(BF16)
    dmix[...] = dot_last(grad_attn, w_proj[...]).astype(BF16)
    heads_back(qkv, probs, mix, dmix, dqkv)
    grad_proj = dot_first(mix[...].astype(BF16), grad_attn).astype(BF16)
    put_block(stage_t, grad_proj, me, 1, 3 * width // PIECES)
    normed = normed1[...]
    h1 = (normed * gain1[...][None, :]).astype(BF16)
    grad = dot_first(h1, dqkv[...]).astype(BF16)
    for j in range(3):
        put_block(stage_t, grad[:, j * width : (j + 1) * width], me, 1, j * width // PIECES)
    t1 = dot_last(dqkv[...], w_qkv[...])
    back1, s_ln1 = norm_back(t1, normed, inv1[...], gain1[...][None, :])
    stage_t[extra[0], rows - EXTRA : rows - EXTRA + 1] = s_ln1.astype(BF16)
    hand_out(stage_t, keep_t, send_t)
    result = grad_mid[...] + back1
    quarter = result.shape[0] // 4
    for i, ref in enumerate((out_a, out_b, out_c, out_d)):
        ref[...] = result[i * quarter : (i + 1) * quarter].reshape(ref.shape).astype(BF16)


def finish_kernel(*refs):
    me, back_a, back_b, back_c, back_d = refs[:5]
    parts = refs[5:-15]
    out, g_ln1, g_qkv, g_proj, g_ln2, g_fc1, g_bfc1, g_fc2 = refs[-15:-7]
    out_near, fc1, fc2, qkv, proj, smalls, sems = refs[-7:]
    half = PIECES // 2
    width, ff = fc1.shape
    rows = width * BLOCKS // PIECES
    thin = width // PIECES
    half_x, half_y = out_near.shape[0] // 2, out_near.shape[1] // 2
    copies = []

    def leave(source, target):
        copies.append(pltpu.make_async_copy(source, target, sems.at[len(copies)]))
        copies[-1].start()

    out_near[half_x:, half_y:] = back_a[...]
    out_near[half_x:, :half_y] = back_b[...]
    out_near[:half_x, half_y:] = back_c[...]
    out_near[:half_x, :half_y] = back_d[...]
    leave(out_near, out)
    total = jnp.zeros((8, width), F32)
    for ref in parts:
        for j in range(ref.shape[0]):
            value = ref[j].astype(F32)
            total = total + jnp.sum((value * value).reshape(-1, 8, width), axis=0)
    total = jnp.sum(jnp.sum(total, axis=0, keepdims=True), axis=1, keepdims=True)
    factor = math.sqrt(param_count(width, ff)) * lax.rsqrt(total)
    per_block = PIECES // BLOCKS
    def spot(core, order, slot):
        piece = core * half + (slot ^ jnp.where(core == 0, me[1 + 2 * order], me[2 + 2 * order]))
        top = pl.multiple_of(piece % per_block * rows, rows)
        left = pl.multiple_of(piece // per_block * width, width)
        return piece, pl.ds(top, rows), pl.ds(left, width)

    for kind in range(2):
        for i, ref in enumerate(parts[4 * kind : 4 * kind + 4]):
            core = me[0] ^ (i // 2)
            for j in range(ref.shape[0]):
                slot = i % 2 * ref.shape[0] + j
                if kind == 0:
                    value = (ref[j].astype(F32) * factor).astype(BF16)
                    piece, down, across = spot(core, 0, slot)
                    fc2[pl.ds(pl.multiple_of(piece * rows, rows), rows), :] = value[:rows]
                    fc1[down, across] = value[rows : 2 * rows]
                else:
                    value = ref[j].astype(F32) * factor
                    piece, down, across = spot(core, 1, slot)
                    for part in range(3):
                        at = slice(part * width, (part + 1) * width)
                        qkv[piece, :, at] = value[part * thin : (part + 1) * thin].astype(BF16)
                    proj[piece] = value[3 * thin : 4 * thin].astype(BF16)
                    smalls[piece] = value[4 * thin :]
        if kind == 0:
            leave(fc2, g_fc2)
            leave(fc1, g_fc1)
        else:
            leave(qkv, g_qkv)
            leave(proj, g_proj)
    g_ln1[...] = smalls[0, 0]
    g_ln2[...] = smalls[1, 0]
    for j in range(BLOCKS):
        g_bfc1[j * width : (j + 1) * width] = smalls[2 + j, 0]
    for copy in copies:
        copy.wait()


def param_count(width, ff):
    return 4 * width * width + 2 * width * ff + 2 * width + ff


VMEM = pl.BlockSpec(memory_space=pltpu.VMEM)
SMEM = pl.BlockSpec(memory_space=pltpu.SMEM)
HBM = pl.BlockSpec(memory_space=pltpu.HBM)


def shape(dims, dtype):
    return jax.ShapeDtypeStruct(dims, dtype)


def like(*arrays):
    return [pltpu.VMEM(a.shape, a.dtype) for a in arrays]


def call(kernel, outs, scratch, flops, me, near, far=(), out_specs=None):
    far = tuple(pltpu.with_memory_space_constraint(a, pltpu.HBM) for a in far)
    args = (me, *near, *far)
    moved = sum(a.size * a.dtype.itemsize for a in args) + sum(
        math.prod(o.shape) * o.dtype.itemsize for o in outs
    )
    return pl.pallas_call(
        kernel,
        out_shape=outs,
        in_specs=[SMEM] + [VMEM] * len(near) + [HBM] * len(far),
        out_specs=out_specs or (VMEM,) * len(outs),
        scratch_shapes=scratch,
        cost_estimate=pl.CostEstimate(flops=flops, bytes_accessed=moved, transcendentals=0),
        compiler_params=pltpu.CompilerParams(vmem_limit_bytes=KERNEL_VMEM),
    )(*args)


def neighbour(shard, step_x, step_y):
    size_x, size_y = lax.axis_size("gx"), lax.axis_size("gy")
    pairs = [
        (x * size_y + y, (x + step_x) % size_x * size_y + (y + step_y) % size_y)
        for x in range(size_x)
        for y in range(size_y)
    ]
    return lax.ppermute(shard, ("gx", "gy"), pairs)


def arriving(tile):
    half_x, half_y = tile.shape[1] // 2, tile.shape[2] // 2
    return (
        neighbour(tile[:, half_x:, :half_y], 0, -1),
        neighbour(tile[:, :half_x, half_y:], -1, 0),
        neighbour(tile[:, :half_x, :half_y], -1, -1),
    )


def window_codes(labels):
    tile_x, tile_y, tile_z = labels.shape
    half_x, half_y = tile_x // 2, tile_y // 2
    last_x = (lax.axis_index("gx") == lax.axis_size("gx") - 1).astype(jnp.int32)
    last_y = (lax.axis_index("gy") == lax.axis_size("gy") - 1).astype(jnp.int32)
    upper_x = (jnp.arange(tile_x) >= half_x).astype(jnp.int32)
    upper_y = (jnp.arange(tile_y) >= half_y).astype(jnp.int32)
    upper_z = (jnp.arange(tile_z) >= tile_z - WZ // 2).astype(jnp.int32)
    codes = (
        labels * 8
        + (4 * last_x) * upper_x[:, None, None]
        + (2 * last_y) * upper_y[None, :, None]
        + upper_z[None, None, :]
    )
    codes = jnp.roll(codes, WZ // 2, axis=2)
    parts = (
        codes[:half_x, :half_y], codes[:half_x, half_y:],
        codes[half_x:, :half_y], codes[half_x:, half_y:],
    )
    return jnp.concatenate([part.reshape(-1) for part in parts])


def swap(shard, flips):
    size_x, size_y = lax.axis_size("gx"), lax.axis_size("gy")
    pairs = [
        (x * size_y + y, (x ^ flips[y % 2][0]) * size_y + (y ^ flips[y % 2][1]))
        for x in range(size_x)
        for y in range(size_y)
    ]
    return lax.ppermute(shard, ("gx", "gy"), pairs)


def add(first, *others):
    total = first.astype(F32)
    for other in others:
        total = total + other.astype(F32)
    return total


SIDE, NEAR, LAYER = (0, 2), (1, 0), (2, 0)
CORE = ((0, 1), (0, 1))
SPARE = 4
ORDERS = (
    ((SIDE, LAYER), (NEAR, SIDE), (LAYER, NEAR)),
    ((NEAR, NEAR), (LAYER, LAYER), (SIDE, SIDE)),
)


def place():
    index_x, index_y = lax.axis_index("gx"), lax.axis_index("gy")
    numbers = [index_y % 2]
    for order in ORDERS:
        for core in range(2):
            number = jnp.int32(0)
            for flips in order:
                flip_x, flip_y = flips[core]
                bit = (index_x & flip_x) if flip_x else (index_y & flip_y)
                number = 2 * number + (bit != 0).astype(jnp.int32)
            numbers.append(number)
    return jnp.stack(numbers)


def fold(keep, got):
    half = keep.shape[0] // 2
    return (
        add(keep[:half], got[:half]).astype(BF16),
        add(keep[half:], got[half:]).astype(BF16),
    )


def after(values, first):
    return lax.optimization_barrier((*values, first))[: len(values)]


def spares():
    for axis in (0, 1):
        spare = SPARE
        while spare < lax.axis_size(("gx", "gy")[axis]):
            yield ((spare, 0) if axis == 0 else (0, spare),) * 2
            spare *= 2


def reduce_all(keep, send, got, keep_t, send_t, away):
    order, order_t = ORDERS
    got_t, = after([swap(send_t, CORE)], send)
    keep_t, send_t = fold(keep_t, got_t)
    for step in range(3):
        got_t = swap(send_t, order_t[step])
        got, = after([got], send_t)
        if step < 2:
            keep, send = fold(keep, got)
            got = swap(send, order[step + 1])
            got_t, = after([got_t], send)
            keep_t, send_t = fold(keep_t, got_t)
        else:
            low = add(keep[0], got[0]).astype(BF16)
            got_t, = after([got_t], low)
            low_t = add(keep_t[0], got_t[0]).astype(BF16)
    for flips in spares():
        got, got_t = swap(low, flips), swap(low_t, flips)
        low = add(low, after([got], low_t)[0]).astype(BF16)
        low_t = add(low_t, after([got_t], low)[0]).astype(BF16)
    parts, parts_t = low[None], low_t[None]
    for step in (2, 1, 0):
        more, more_t = swap(parts, order[step]), swap(parts_t, order_t[step])
        if step == 0:
            away = after(away, parts)
            back = [neighbour(away[0], 0, 1), neighbour(away[1], 1, 0), neighbour(away[2], 1, 1)]
            more, more_t, *back = lax.optimization_barrier((more, more_t, *back))
            break
        more, more_t = lax.optimization_barrier((more, more_t))
        parts, parts_t = jnp.concatenate([parts, more]), jnp.concatenate([parts_t, more_t])
    streams = ((parts, more), (parts_t, more_t))
    return back, [part for pair in streams for part in (*pair, swap(pair[0], CORE), swap(pair[1], CORE))]


def body(tokens, upstream, window_labels, ln1_gain, w_qkv, w_proj, ln2_gain, w_fc1, b_fc1, w_fc2):
    width, ff = w_fc1.shape
    heads = width // HD
    parts = arriving(jnp.stack([tokens, upstream]))
    codes = window_codes(window_labels)
    rows = codes.shape[0]
    me = place()
    piece = BLOCKS * width // PIECES
    thin = width // PIECES
    rows_f, rows_t = 2 * piece, 4 * thin + EXTRA
    half = shape((PIECES // 2, rows_f, width), BF16)
    half_t = shape((PIECES // 2, rows_t, width), BF16)
    weights = (w_qkv, w_proj)
    weights = call(
        fetch_kernel, tuple(shape(w.shape, BF16) for w in weights), [pltpu.SemaphoreType.DMA((2,))], 0, me, (), weights
    )
    w_qkv, w_proj = weights
    parts = after(parts, w_proj)
    keep, send, *saved = call(
        forward_kernel,
        (half, half)
        + (shape((1 + BLOCKS, width), F32), shape((rows, width), F32), shape((rows, width), F32), shape((rows, 1), F32))
        + (shape((rows, 3 * width), BF16), shape((heads, rows, rows), BF16), shape((rows, width), F32)),
        [pltpu.VMEM((rows, rows), F32), pltpu.VMEM((PIECES, rows_f, width), BF16), pltpu.VMEM((rows, ff), F32), pltpu.VMEM((rows, ff), F32), pltpu.VMEM((rows, ff), BF16), pltpu.VMEM((rows, ff), BF16)]
        + like(w_fc1, w_fc2)
        + [pltpu.SemaphoreType.DMA((2,))],
        2 * rows * width * (4 * width + 5 * ff) + 4 * heads * rows * rows * LANES,
        me,
        (tokens, upstream, *parts, codes[:, None], codes[None, :], ln1_gain, ln2_gain, b_fc1, w_qkv, w_proj),
        (w_fc1, w_fc2),
    )
    quarter = shape(parts[0].shape[1:], BF16)
    small, grad_mid, normed1, inv1, qkv, probs, mix = saved
    got = swap(send, CORE)
    *done, keep_t, send_t = call(
        backward_kernel,
        (quarter,) * 4 + (half_t, half_t),
        [
            pltpu.VMEM((rows, width), BF16),
            pltpu.VMEM((rows, 3 * width), BF16),
            pltpu.VMEM((PIECES, rows_t, width), BF16),
        ],
        2 * rows * width * 8 * width + 8 * heads * rows * rows * LANES,
        me,
        (small, grad_mid, normed1, inv1, qkv, probs, mix, ln1_gain, w_qkv, w_proj),
    )
    got, = after([got], keep_t)
    keep, send = fold(keep, got)
    got = swap(send, ORDERS[0][0])
    back, slots = reduce_all(keep, send, got, keep_t, send_t, done[1:])
    result, g_ln1, g_qkv, g_proj, g_ln2, g_fc1, g_bfc1, g_fc2 = call(
        finish_kernel,
        (
            shape(tokens.shape, BF16), shape((width,), F32), shape((PIECES, thin, 3 * width), BF16),
            shape((PIECES, thin, width), BF16), shape((width,), F32), shape((width, ff), BF16),
            shape((ff,), F32), shape((ff, width), BF16),
        ),
        like(tokens, w_fc1, w_fc2)
        + [
            pltpu.VMEM((PIECES, thin, 3 * width), BF16),
            pltpu.VMEM((PIECES, thin, width), BF16),
            pltpu.VMEM((PIECES, EXTRA, width), F32),
            pltpu.SemaphoreType.DMA((5,)),
        ],
        4 * width * width,
        me,
        (done[0], *back, *slots),
        out_specs=(HBM, VMEM, HBM, HBM, VMEM, HBM, VMEM, HBM),
    )
    g_qkv, g_proj = g_qkv.reshape(width, 3 * width), g_proj.reshape(width, width)
    return (result, g_ln1, g_qkv, g_proj, g_ln2, g_fc1, g_bfc1, g_fc2)


def solution(mesh):
    return jax.shard_map(
        body,
        mesh=mesh,
        in_specs=(
            P("gx", "gy", None, None),
            P("gx", "gy", None, None),
            P("gx", "gy", None),
            P(), P(), P(), P(), P(), P(), P(),
        ),
        out_specs=(P("gx", "gy", None, None), P(), P(), P(), P(), P(), P(), P()),
        check_vma=False,
    )
```

```python
import functools
import math

import jax
import jax.numpy as jnp
from jax import lax
from jax.experimental import pallas as pl
from jax.experimental.pallas import tpu as pltpu
from jax.sharding import PartitionSpec as P

HD = 32
WZ = 8
EPS = 1e-05
CUBIC = 0.044715
ROOT_TWO_PI = math.sqrt(2.0 / math.pi)
LOG2_E = 1.0 / math.log(2.0)
LANES = 128
PIECES = 16
BLOCKS = 4
EXTRA = 8
KERNEL_VMEM = 40 << 20
F32 = jnp.float32
BF16 = jnp.bfloat16


def dot(a, b):
    return jnp.dot(a, b, preferred_element_type=F32)


def dot_last(a, b):
    return lax.dot_general(a, b, (((1,), (1,)), ((), ())), preferred_element_type=F32)


def dot_first(a, b):
    return lax.dot_general(a, b, (((0,), (0,)), ((), ())), preferred_element_type=F32)


def row_stats(values):
    row_mean = jnp.mean(values, axis=-1, keepdims=True)
    center = values - row_mean
    variance = jnp.mean(center * center, axis=-1, keepdims=True)
    inv_std = lax.rsqrt(variance + EPS)
    return (center * inv_std, inv_std)


def norm_back(incoming, normed, inv_std, gain_vec):
    terms = incoming * normed
    scaled = incoming * gain_vec
    first_mean = jnp.mean(scaled, axis=-1, keepdims=True)
    second_mean = jnp.mean(terms * gain_vec, axis=-1, keepdims=True)
    back = inv_std * (scaled - first_mean - normed * second_mean)
    return (back, jnp.sum(terms, axis=0, keepdims=True))


def head_columns(qkv, head, width):
    group, sub = divmod(head, LANES // HD)
    lo = group * LANES
    mine = lax.broadcasted_iota(jnp.int32, (1, LANES), 1) // HD == sub
    q, k, v = (qkv[:, i * width + lo : i * width + lo + LANES] for i in range(3))
    return (lo, sub, mine, q, k, v)


def low_slot(piece, me, order):
    half = PIECES // 2
    return (piece % half) ^ me[1 + 2 * order + piece // half]


def put_block(stage, value, me, order, top, first=0, pieces=PIECES):
    rows = value.shape[0] // pieces
    for i in range(pieces):
        piece = first + i
        core = piece // (PIECES // 2)
        slot = (core ^ me[0]) * (PIECES // 2) + low_slot(piece, me, order)
        stage[slot, top : top + rows] = value[i * rows : (i + 1) * rows]


def hand_out(stage, keep, send):
    half = stage.shape[0] // 2
    keep[...] = stage[:half]
    send[...] = stage[half:]


def load_window(own, parts, index):
    half_x, half_y = own.shape[0] // 2, own.shape[1] // 2
    rows = [own[half_x:, half_y:]] + [part[index] for part in parts]
    return jnp.concatenate([r.astype(F32).reshape(-1, r.shape[-1]) for r in rows], axis=0)


def fetch_kernel(*refs):
    count = (len(refs) - 2) // 2
    copies = [
        pltpu.make_async_copy(refs[1 + i], refs[1 + count + i], refs[-1].at[i]) for i in range(count)
    ]
    for copy in copies:
        copy.start()
    for copy in copies:
        copy.wait()


def forward_kernel(
    me, tok, up_own, part_b, part_c, part_d, code_col, code_row,
    gain1, gain2, b_fc1, w_qkv, w_proj, w_fc1_far, w_fc2_far,
    keep, send, small, grad_mid, normed1, inv1, qkv, probs, mix,
    allowed, stage, pre_all, up_hidden, hidden_all, grad_pre, w_fc1, w_fc2, sems,
):
    fetch = [
        pltpu.make_async_copy(w_fc1_far, w_fc1, sems.at[0]),
        pltpu.make_async_copy(w_fc2_far, w_fc2, sems.at[1]),
    ]
    for copy in fetch:
        copy.start()
    width = w_proj.shape[0]
    heads = width // HD
    rows = allowed.shape[0]
    each = PIECES // BLOCKS
    piece = each * width * BLOCKS // (PIECES * each)
    parts = (part_b, part_c, part_d)
    x = load_window(tok, parts, 0)
    normed, inv = row_stats(x)
    normed1[...] = normed
    inv1[...] = inv
    h1 = (normed * gain1[...][None, :]).astype(BF16)
    qkv[...] = dot(h1, w_qkv[...]).astype(BF16)
    allowed[...] = (code_col[...] == code_row[...]).astype(F32)

    together = 4
    for first in range(0, heads, together):
        masks = []
        for head in range(first, first + together):
            lo, sub, mine, q, k, v = head_columns(qkv, head, width)
            masks.append(mine)
        stacked = jnp.concatenate([jnp.where(mine, q, jnp.zeros_like(q)) for mine in masks], axis=0)
        scores = dot_last(stacked, k).reshape(together, rows, rows)
        scores = jnp.where(allowed[...][None] > 0.0, scores, -1e30)
        highest = jnp.max(scores, axis=-1, keepdims=True)
        weight = jnp.exp2((scores - highest) * (HD ** (-0.5) * LOG2_E))
        total = jnp.sum(weight, axis=-1, keepdims=True)
        prob = (weight * (1.0 / total)).astype(BF16)
        probs[first : first + together] = prob
        part = dot(prob.reshape(together * rows, rows), v).reshape(together, rows, LANES)
        for i, mine in enumerate(masks):
            old = mix[:, lo : lo + LANES] if (first + i) % (LANES // HD) else None
            mix[:, lo : lo + LANES] = part[i] if old is None else jnp.where(mine, part[i], old)

    for copy in fetch:
        copy.wait()
    mix_low = mix[...].astype(BF16)
    mid = (x + dot(mix_low, w_proj[...])).astype(BF16).astype(F32)
    normed2, inv2 = row_stats(mid)
    h2 = (normed2 * gain2[...][None, :]).astype(BF16)
    up = load_window(up_own, parts, 1)
    up_low = up.astype(BF16)

    pre_all[...] = dot(h2, w_fc1[...])
    up_hidden[...] = dot_last(up_low, w_fc2[...])
    count = pre_all.shape[0]
    chunk = 32
    bias = b_fc1[...][None, :]
    total = None
    for i in range(count // chunk):
        at = slice(i * chunk, (i + 1) * chunk)
        pre = pre_all[at, :] + bias
        square = pre * pre
        tanh_value = jnp.tanh(pre * (ROOT_TWO_PI + (ROOT_TWO_PI * CUBIC) * square))
        half = 0.5 + 0.5 * tanh_value
        hidden_all[at, :] = (pre * half).astype(BF16)
        slope = half + pre * (1.0 - tanh_value * tanh_value) * (
            0.5 * ROOT_TWO_PI + (1.5 * ROOT_TWO_PI * CUBIC) * square
        )
        gp = (up_hidden[at, :] * slope).astype(BF16)
        grad_pre[at, :] = gp
        part = jnp.sum(gp.astype(F32).reshape(chunk // 8, 8, -1), axis=0)
        total = part if total is None else total + part
    total = jnp.sum(total, axis=0, keepdims=True)
    for j in range(BLOCKS):
        small[1 + j : 2 + j, :] = total[:, j * width : (j + 1) * width]
    put_block(stage, dot_first(hidden_all[...], up_low).astype(BF16), me, 0, 0)
    t2 = dot_last(grad_pre[...], w_fc1[...])
    grad = dot_first(h2, grad_pre[...]).astype(BF16)
    for j in range(BLOCKS):
        put_block(stage, grad[:, j * width : (j + 1) * width], me, 0, piece, j * each, each)
    back2, s_ln2 = norm_back(t2, normed2, inv2, gain2[...][None, :])
    small[0:1, :] = s_ln2
    grad_mid[...] = up + back2
    hand_out(stage, keep, send)


def heads_back(qkv, probs, mix, dmix, dqkv):
    width = mix.shape[1]
    score_scale = HD ** (-0.5)
    per_group = LANES // HD
    for group in range(width // LANES):
        sums = None
        together = 4
        for first in range(group * per_group, (group + 1) * per_group, together):
            masks, deltas, dos = [], [], []
            for head in range(first, first + together):
                lo, sub, mine, q, k, v = head_columns(qkv, head, width)
                do = dmix[:, lo : lo + LANES]
                do_mine = jnp.where(mine, do, jnp.zeros_like(do))
                deltas.append(jnp.sum(do_mine.astype(F32) * mix[:, lo : lo + LANES], axis=-1, keepdims=True))
                masks.append(mine)
                dos.append(do_mine)
            rows = do.shape[0]
            prob = probs[first : first + together]
            dp = dot_last(jnp.concatenate(dos, axis=0), v).reshape(together, rows, rows)
            ds = (prob.astype(F32) * (dp - jnp.stack(deltas))).astype(BF16)
            dq = dot(ds.reshape(together * rows, rows), k).reshape(together, rows, LANES)
            for i, mine in enumerate(masks):
                parts = (dq[i] * score_scale, dot_first(ds[i], q) * score_scale, dot_first(prob[i], do))
                sums = parts if sums is None else [jnp.where(mine, a, b) for a, b in zip(parts, sums)]
        for i, part in enumerate(sums):
            dqkv[:, i * width + lo : i * width + lo + LANES] = part.astype(BF16)


def backward_kernel(
    me, small, grad_mid, normed1, inv1, qkv, probs, mix, gain1, w_qkv, w_proj,
    out_a, out_b, out_c, out_d, keep_t, send_t,
    dmix, dqkv, stage_t,
):
    width = mix.shape[1]
    pieces, rows, _ = stage_t.shape
    stage_t[:, rows - EXTRA :] = jnp.zeros((pieces, EXTRA, width), BF16)
    extra = [me[0] * (PIECES // 2) + low_slot(i, me, 1) for i in range(BLOCKS + 2)]
    for i in range(BLOCKS + 1):
        stage_t[extra[i + 1], rows - EXTRA : rows - EXTRA + 1] = small[i : i + 1, :].astype(BF16)
    grad_attn = grad_mid[...].astype(BF16)
    dmix[...] = dot_last(grad_attn, w_proj[...]).astype(BF16)
    heads_back(qkv, probs, mix, dmix, dqkv)
    grad_proj = dot_first(mix[...].astype(BF16), grad_attn).astype(BF16)
    put_block(stage_t, grad_proj, me, 1, 3 * width // PIECES)
    normed = normed1[...]
    h1 = (normed * gain1[...][None, :]).astype(BF16)
    grad = dot_first(h1, dqkv[...]).astype(BF16)
    for j in range(3):
        put_block(stage_t, grad[:, j * width : (j + 1) * width], me, 1, j * width // PIECES)
    t1 = dot_last(dqkv[...], w_qkv[...])
    back1, s_ln1 = norm_back(t1, normed, inv1[...], gain1[...][None, :])
    stage_t[extra[0], rows - EXTRA : rows - EXTRA + 1] = s_ln1.astype(BF16)
    hand_out(stage_t, keep_t, send_t)
    result = grad_mid[...] + back1
    quarter = result.shape[0] // 4
    for i, ref in enumerate((out_a, out_b, out_c, out_d)):
        ref[...] = result[i * quarter : (i + 1) * quarter].reshape(ref.shape).astype(BF16)


def finish_kernel(*refs):
    me, back_a, back_b, back_c, back_d = refs[:5]
    parts = refs[5:-15]
    out, g_ln1, g_qkv, g_proj, g_ln2, g_fc1, g_bfc1, g_fc2 = refs[-15:-7]
    out_near, fc1, fc2, qkv, proj, smalls, sems = refs[-7:]
    half = PIECES // 2
    width, ff = fc1.shape
    rows = width * BLOCKS // PIECES
    thin = width // PIECES
    half_x, half_y = out_near.shape[0] // 2, out_near.shape[1] // 2
    copies = []

    def leave(source, target):
        copies.append(pltpu.make_async_copy(source, target, sems.at[len(copies)]))
        copies[-1].start()

    out_near[half_x:, half_y:] = back_a[...]
    out_near[half_x:, :half_y] = back_b[...]
    out_near[:half_x, half_y:] = back_c[...]
    out_near[:half_x, :half_y] = back_d[...]
    leave(out_near, out)
    total = jnp.zeros((8, width), F32)
    for ref in parts:
        for j in range(ref.shape[0]):
            value = ref[j].astype(F32)
            total = total + jnp.sum((value * value).reshape(-1, 8, width), axis=0)
    total = jnp.sum(jnp.sum(total, axis=0, keepdims=True), axis=1, keepdims=True)
    factor = math.sqrt(param_count(width, ff)) * lax.rsqrt(total)
    per_block = PIECES // BLOCKS
    def spot(core, order, slot):
        piece = core * half + (slot ^ jnp.where(core == 0, me[1 + 2 * order], me[2 + 2 * order]))
        top = pl.multiple_of(piece % per_block * rows, rows)
        left = pl.multiple_of(piece // per_block * width, width)
        return piece, pl.ds(top, rows), pl.ds(left, width)

    for kind in range(2):
        for i, ref in enumerate(parts[4 * kind : 4 * kind + 4]):
            core = me[0] ^ (i // 2)
            for j in range(ref.shape[0]):
                slot = i % 2 * ref.shape[0] + j
                if kind == 0:
                    value = (ref[j].astype(F32) * factor).astype(BF16)
                    piece, down, across = spot(core, 0, slot)
                    fc2[pl.ds(pl.multiple_of(piece * rows, rows), rows), :] = value[:rows]
                    fc1[down, across] = value[rows : 2 * rows]
                else:
                    value = ref[j].astype(F32) * factor
                    piece, down, across = spot(core, 1, slot)
                    for part in range(3):
                        at = slice(part * width, (part + 1) * width)
                        qkv[piece, :, at] = value[part * thin : (part + 1) * thin].astype(BF16)
                    proj[piece] = value[3 * thin : 4 * thin].astype(BF16)
                    smalls[piece] = value[4 * thin :]
        if kind == 0:
            leave(fc2, g_fc2)
            leave(fc1, g_fc1)
        else:
            leave(qkv, g_qkv)
            leave(proj, g_proj)
    g_ln1[...] = smalls[0, 0]
    g_ln2[...] = smalls[1, 0]
    for j in range(BLOCKS):
        g_bfc1[j * width : (j + 1) * width] = smalls[2 + j, 0]
    for copy in copies:
        copy.wait()


def param_count(width, ff):
    return 4 * width * width + 2 * width * ff + 2 * width + ff


VMEM = pl.BlockSpec(memory_space=pltpu.VMEM)
SMEM = pl.BlockSpec(memory_space=pltpu.SMEM)
HBM = pl.BlockSpec(memory_space=pltpu.HBM)


def shape(dims, dtype):
    return jax.ShapeDtypeStruct(dims, dtype)


def like(*arrays):
    return [pltpu.VMEM(a.shape, a.dtype) for a in arrays]


def call(kernel, outs, scratch, flops, me, near, far=(), out_specs=None):
    far = tuple(pltpu.with_memory_space_constraint(a, pltpu.HBM) for a in far)
    args = (me, *near, *far)
    moved = sum(a.size * a.dtype.itemsize for a in args) + sum(
        math.prod(o.shape) * o.dtype.itemsize for o in outs
    )
    return pl.pallas_call(
        kernel,
        out_shape=outs,
        in_specs=[SMEM] + [VMEM] * len(near) + [HBM] * len(far),
        out_specs=out_specs or (VMEM,) * len(outs),
        scratch_shapes=scratch,
        cost_estimate=pl.CostEstimate(flops=flops, bytes_accessed=moved, transcendentals=0),
        compiler_params=pltpu.CompilerParams(vmem_limit_bytes=KERNEL_VMEM),
    )(*args)


def neighbour(shard, step_x, step_y):
    size_x, size_y = lax.axis_size("gx"), lax.axis_size("gy")
    pairs = [
        (x * size_y + y, (x + step_x) % size_x * size_y + (y + step_y) % size_y)
        for x in range(size_x)
        for y in range(size_y)
    ]
    return lax.ppermute(shard, ("gx", "gy"), pairs)


def arriving(tile):
    half_x, half_y = tile.shape[1] // 2, tile.shape[2] // 2
    return (
        neighbour(tile[:, half_x:, :half_y], 0, -1),
        neighbour(tile[:, :half_x, half_y:], -1, 0),
        neighbour(tile[:, :half_x, :half_y], -1, -1),
    )


def window_codes(labels):
    tile_x, tile_y, tile_z = labels.shape
    half_x, half_y = tile_x // 2, tile_y // 2
    last_x = (lax.axis_index("gx") == lax.axis_size("gx") - 1).astype(jnp.int32)
    last_y = (lax.axis_index("gy") == lax.axis_size("gy") - 1).astype(jnp.int32)
    upper_x = (jnp.arange(tile_x) >= half_x).astype(jnp.int32)
    upper_y = (jnp.arange(tile_y) >= half_y).astype(jnp.int32)
    upper_z = (jnp.arange(tile_z) >= tile_z - WZ // 2).astype(jnp.int32)
    codes = (
        labels * 8
        + (4 * last_x) * upper_x[:, None, None]
        + (2 * last_y) * upper_y[None, :, None]
        + upper_z[None, None, :]
    )
    codes = jnp.roll(codes, WZ // 2, axis=2)
    parts = (
        codes[:half_x, :half_y], codes[:half_x, half_y:],
        codes[half_x:, :half_y], codes[half_x:, half_y:],
    )
    return jnp.concatenate([part.reshape(-1) for part in parts])


def swap(shard, flips):
    size_x, size_y = lax.axis_size("gx"), lax.axis_size("gy")
    pairs = [
        (x * size_y + y, (x ^ flips[y % 2][0]) * size_y + (y ^ flips[y % 2][1]))
        for x in range(size_x)
        for y in range(size_y)
    ]
    return lax.ppermute(shard, ("gx", "gy"), pairs)


def add(first, *others):
    total = first.astype(F32)
    for other in others:
        total = total + other.astype(F32)
    return total


SIDE, NEAR, LAYER = (0, 2), (1, 0), (2, 0)
CORE = ((0, 1), (0, 1))
SPARE = 4
ORDERS = (
    ((SIDE, LAYER), (NEAR, SIDE), (LAYER, NEAR)),
    ((NEAR, NEAR), (LAYER, LAYER), (SIDE, SIDE)),
)


def place():
    index_x, index_y = lax.axis_index("gx"), lax.axis_index("gy")
    numbers = [index_y % 2]
    for order in ORDERS:
        for core in range(2):
            number = jnp.int32(0)
            for flips in order:
                flip_x, flip_y = flips[core]
                bit = (index_x & flip_x) if flip_x else (index_y & flip_y)
                number = 2 * number + (bit != 0).astype(jnp.int32)
            numbers.append(number)
    return jnp.stack(numbers)


def fold(keep, got):
    half = keep.shape[0] // 2
    return (
        add(keep[:half], got[:half]).astype(BF16),
        add(keep[half:], got[half:]).astype(BF16),
    )


def after(values, first):
    return lax.optimization_barrier((*values, first))[: len(values)]


def spares():
    for axis in (0, 1):
        spare = SPARE
        while spare < lax.axis_size(("gx", "gy")[axis]):
            yield ((spare, 0) if axis == 0 else (0, spare),) * 2
            spare *= 2


def reduce_all(keep, send, got, keep_t, send_t, away):
    order, order_t = ORDERS
    got_t, = after([swap(send_t, CORE)], send)
    keep_t, send_t = fold(keep_t, got_t)
    homes, back = ((0, 1), (1, 0), (1, 1)), []
    for step in range(3):
        got_t = swap(send_t, order_t[step])
        if step < 2:
            got, home = after([got, neighbour(away[step], *homes[step])], send_t)
            back.append(home)
        else:
            got, = after([got], send_t)
        if step < 2:
            keep, send = fold(keep, got)
            got = swap(send, order[step + 1])
            got_t, = after([got_t], send)
            keep_t, send_t = fold(keep_t, got_t)
        else:
            low = add(keep[0], got[0]).astype(BF16)
            got_t, = after([got_t], low)
            low_t = add(keep_t[0], got_t[0]).astype(BF16)
    for flips in spares():
        got, got_t = swap(low, flips), swap(low_t, flips)
        if len(back) == 2:
            got, home = lax.optimization_barrier((got, neighbour(away[2], *homes[2])))
            back.append(home)
        low = add(low, after([got], low_t)[0]).astype(BF16)
        low_t = add(low_t, after([got_t], low)[0]).astype(BF16)
    parts, parts_t = low[None], low_t[None]
    for step in (2, 1, 0):
        more, more_t = swap(parts, order[step]), swap(parts_t, order_t[step])
        if step == 0:
            more, more_t = lax.optimization_barrier((more, more_t))
            break
        more, more_t = lax.optimization_barrier((more, more_t))
        parts, parts_t = jnp.concatenate([parts, more]), jnp.concatenate([parts_t, more_t])
    streams = ((parts, more), (parts_t, more_t))
    return back, [part for pair in streams for part in (*pair, swap(pair[0], CORE), swap(pair[1], CORE))]


def body(tokens, upstream, window_labels, ln1_gain, w_qkv, w_proj, ln2_gain, w_fc1, b_fc1, w_fc2):
    width, ff = w_fc1.shape
    heads = width // HD
    parts = arriving(jnp.stack([tokens, upstream]))
    codes = window_codes(window_labels)
    rows = codes.shape[0]
    me = place()
    piece = BLOCKS * width // PIECES
    thin = width // PIECES
    rows_f, rows_t = 2 * piece, 4 * thin + EXTRA
    half = shape((PIECES // 2, rows_f, width), BF16)
    half_t = shape((PIECES // 2, rows_t, width), BF16)
    weights = (w_qkv, w_proj)
    weights = call(
        fetch_kernel, tuple(shape(w.shape, BF16) for w in weights), [pltpu.SemaphoreType.DMA((2,))], 0, me, (), weights
    )
    w_qkv, w_proj = weights
    parts = after(parts, w_proj)
    keep, send, *saved = call(
        forward_kernel,
        (half, half)
        + (shape((1 + BLOCKS, width), F32), shape((rows, width), F32), shape((rows, width), F32), shape((rows, 1), F32))
        + (shape((rows, 3 * width), BF16), shape((heads, rows, rows), BF16), shape((rows, width), F32)),
        [pltpu.VMEM((rows, rows), F32), pltpu.VMEM((PIECES, rows_f, width), BF16), pltpu.VMEM((rows, ff), F32), pltpu.VMEM((rows, ff), F32), pltpu.VMEM((rows, ff), BF16), pltpu.VMEM((rows, ff), BF16)]
        + like(w_fc1, w_fc2)
        + [pltpu.SemaphoreType.DMA((2,))],
        2 * rows * width * (4 * width + 5 * ff) + 4 * heads * rows * rows * LANES,
        me,
        (tokens, upstream, *parts, codes[:, None], codes[None, :], ln1_gain, ln2_gain, b_fc1, w_qkv, w_proj),
        (w_fc1, w_fc2),
    )
    quarter = shape(parts[0].shape[1:], BF16)
    small, grad_mid, normed1, inv1, qkv, probs, mix = saved
    got = swap(send, CORE)
    *done, keep_t, send_t = call(
        backward_kernel,
        (quarter,) * 4 + (half_t, half_t),
        [
            pltpu.VMEM((rows, width), BF16),
            pltpu.VMEM((rows, 3 * width), BF16),
            pltpu.VMEM((PIECES, rows_t, width), BF16),
        ],
        2 * rows * width * 8 * width + 8 * heads * rows * rows * LANES,
        me,
        (small, grad_mid, normed1, inv1, qkv, probs, mix, ln1_gain, w_qkv, w_proj),
    )
    got, = after([got], keep_t)
    keep, send = fold(keep, got)
    got = swap(send, ORDERS[0][0])
    back, slots = reduce_all(keep, send, got, keep_t, send_t, done[1:])
    result, g_ln1, g_qkv, g_proj, g_ln2, g_fc1, g_bfc1, g_fc2 = call(
        finish_kernel,
        (
            shape(tokens.shape, BF16), shape((width,), F32), shape((PIECES, thin, 3 * width), BF16),
            shape((PIECES, thin, width), BF16), shape((width,), F32), shape((width, ff), BF16),
            shape((ff,), F32), shape((ff, width), BF16),
        ),
        like(tokens, w_fc1, w_fc2)
        + [
            pltpu.VMEM((PIECES, thin, 3 * width), BF16),
            pltpu.VMEM((PIECES, thin, width), BF16),
            pltpu.VMEM((PIECES, EXTRA, width), F32),
            pltpu.SemaphoreType.DMA((5,)),
        ],
        4 * width * width,
        me,
        (done[0], *back, *slots),
        out_specs=(HBM, VMEM, HBM, HBM, VMEM, HBM, VMEM, HBM),
    )
    g_qkv, g_proj = g_qkv.reshape(width, 3 * width), g_proj.reshape(width, width)
    return (result, g_ln1, g_qkv, g_proj, g_ln2, g_fc1, g_bfc1, g_fc2)


def solution(mesh):
    return jax.shard_map(
        body,
        mesh=mesh,
        in_specs=(
            P("gx", "gy", None, None),
            P("gx", "gy", None, None),
            P("gx", "gy", None),
            P(), P(), P(), P(), P(), P(), P(),
        ),
        out_specs=(P("gx", "gy", None, None), P(), P(), P(), P(), P(), P(), P()),
        check_vma=False,
    )
```

```python
import functools
import math

import jax
import jax.numpy as jnp
from jax import lax
from jax.experimental import pallas as pl
from jax.experimental.pallas import tpu as pltpu
from jax.sharding import PartitionSpec as P

HD = 32
WZ = 8
EPS = 1e-05
CUBIC = 0.044715
ROOT_TWO_PI = math.sqrt(2.0 / math.pi)
LOG2_E = 1.0 / math.log(2.0)
LANES = 128
PIECES = 16
BLOCKS = 4
EXTRA = 8
KERNEL_VMEM = 40 << 20
F32 = jnp.float32
BF16 = jnp.bfloat16


def dot(a, b):
    return jnp.dot(a, b, preferred_element_type=F32)


def dot_last(a, b):
    return lax.dot_general(a, b, (((1,), (1,)), ((), ())), preferred_element_type=F32)


def dot_first(a, b):
    return lax.dot_general(a, b, (((0,), (0,)), ((), ())), preferred_element_type=F32)


def row_stats(values):
    row_mean = jnp.mean(values, axis=-1, keepdims=True)
    center = values - row_mean
    variance = jnp.mean(center * center, axis=-1, keepdims=True)
    inv_std = lax.rsqrt(variance + EPS)
    return (center * inv_std, inv_std)


def norm_back(incoming, normed, inv_std, gain_vec):
    terms = incoming * normed
    scaled = incoming * gain_vec
    first_mean = jnp.mean(scaled, axis=-1, keepdims=True)
    second_mean = jnp.mean(terms * gain_vec, axis=-1, keepdims=True)
    back = inv_std * (scaled - first_mean - normed * second_mean)
    return (back, jnp.sum(terms, axis=0, keepdims=True))


def head_columns(qkv, head, width):
    group, sub = divmod(head, LANES // HD)
    lo = group * LANES
    mine = lax.broadcasted_iota(jnp.int32, (1, LANES), 1) // HD == sub
    q, k, v = (qkv[:, i * width + lo : i * width + lo + LANES] for i in range(3))
    return (lo, sub, mine, q, k, v)


def low_slot(piece, me, order):
    half = PIECES // 2
    return (piece % half) ^ me[1 + 2 * order + piece // half]


def put_block(stage, value, me, order, top, first=0, pieces=PIECES):
    rows = value.shape[0] // pieces
    for i in range(pieces):
        piece = first + i
        core = piece // (PIECES // 2)
        slot = (core ^ me[0]) * (PIECES // 2) + low_slot(piece, me, order)
        stage[slot, top : top + rows] = value[i * rows : (i + 1) * rows]


def hand_out(stage, keep, send):
    half = stage.shape[0] // 2
    keep[...] = stage[:half]
    send[...] = stage[half:]


def load_window(own, parts, index):
    half_x, half_y = own.shape[0] // 2, own.shape[1] // 2
    rows = [own[half_x:, half_y:]] + [part[index] for part in parts]
    return jnp.concatenate([r.astype(F32).reshape(-1, r.shape[-1]) for r in rows], axis=0)


def fetch_kernel(*refs):
    count = (len(refs) - 2) // 2
    copies = [
        pltpu.make_async_copy(refs[1 + i], refs[1 + count + i], refs[-1].at[i]) for i in range(count)
    ]
    for copy in copies:
        copy.start()
    for copy in copies:
        copy.wait()


def forward_kernel(
    me, tok, up_own, part_b, part_c, part_d, code_col, code_row,
    gain1, gain2, b_fc1, w_qkv, w_proj, w_fc1_far, w_fc2_far,
    keep, send, small, grad_mid, normed1, inv1, qkv, probs, mix,
    allowed, stage, pre_all, up_hidden, hidden_all, grad_pre, w_fc1, w_fc2, sems,
):
    fetch = [
        pltpu.make_async_copy(w_fc1_far, w_fc1, sems.at[0]),
        pltpu.make_async_copy(w_fc2_far, w_fc2, sems.at[1]),
    ]
    for copy in fetch:
        copy.start()
    width = w_proj.shape[0]
    heads = width // HD
    rows = allowed.shape[0]
    each = PIECES // BLOCKS
    piece = each * width * BLOCKS // (PIECES * each)
    parts = (part_b, part_c, part_d)
    x = load_window(tok, parts, 0)
    normed, inv = row_stats(x)
    normed1[...] = normed
    inv1[...] = inv
    h1 = (normed * gain1[...][None, :]).astype(BF16)
    qkv[...] = dot(h1, w_qkv[...]).astype(BF16)
    allowed[...] = (code_col[...] == code_row[...]).astype(F32)

    together = 4
    for first in range(0, heads, together):
        masks = []
        for head in range(first, first + together):
            lo, sub, mine, q, k, v = head_columns(qkv, head, width)
            masks.append(mine)
        stacked = jnp.concatenate([jnp.where(mine, q, jnp.zeros_like(q)) for mine in masks], axis=0)
        scores = dot_last(stacked, k).reshape(together, rows, rows)
        scores = jnp.where(allowed[...][None] > 0.0, scores, -1e30)
        highest = jnp.max(scores, axis=-1, keepdims=True)
        weight = jnp.exp2((scores - highest) * (HD ** (-0.5) * LOG2_E))
        total = jnp.sum(weight, axis=-1, keepdims=True)
        prob = (weight * (1.0 / total)).astype(BF16)
        probs[first : first + together] = prob
        part = dot(prob.reshape(together * rows, rows), v).reshape(together, rows, LANES)
        for i, mine in enumerate(masks):
            old = mix[:, lo : lo + LANES] if (first + i) % (LANES // HD) else None
            mix[:, lo : lo + LANES] = part[i] if old is None else jnp.where(mine, part[i], old)

    for copy in fetch:
        copy.wait()
    mix_low = mix[...].astype(BF16)
    mid = (x + dot(mix_low, w_proj[...])).astype(BF16).astype(F32)
    normed2, inv2 = row_stats(mid)
    h2 = (normed2 * gain2[...][None, :]).astype(BF16)
    up = load_window(up_own, parts, 1)
    up_low = up.astype(BF16)

    pre_all[...] = dot(h2, w_fc1[...])
    up_hidden[...] = dot_last(up_low, w_fc2[...])
    count = pre_all.shape[0]
    chunk = 32
    bias = b_fc1[...][None, :]
    total = None
    for i in range(count // chunk):
        at = slice(i * chunk, (i + 1) * chunk)
        pre = pre_all[at, :] + bias
        square = pre * pre
        tanh_value = jnp.tanh(pre * (ROOT_TWO_PI + (ROOT_TWO_PI * CUBIC) * square))
        half = 0.5 + 0.5 * tanh_value
        hidden_all[at, :] = (pre * half).astype(BF16)
        slope = half + pre * (1.0 - tanh_value * tanh_value) * (
            0.5 * ROOT_TWO_PI + (1.5 * ROOT_TWO_PI * CUBIC) * square
        )
        gp = (up_hidden[at, :] * slope).astype(BF16)
        grad_pre[at, :] = gp
        part = jnp.sum(gp.astype(F32).reshape(chunk // 8, 8, -1), axis=0)
        total = part if total is None else total + part
    total = jnp.sum(total, axis=0, keepdims=True)
    for j in range(BLOCKS):
        small[1 + j : 2 + j, :] = total[:, j * width : (j + 1) * width]
    put_block(stage, dot_first(hidden_all[...], up_low).astype(BF16), me, 0, 0)
    t2 = dot_last(grad_pre[...], w_fc1[...])
    grad = dot_first(h2, grad_pre[...]).astype(BF16)
    for j in range(BLOCKS):
        put_block(stage, grad[:, j * width : (j + 1) * width], me, 0, piece, j * each, each)
    back2, s_ln2 = norm_back(t2, normed2, inv2, gain2[...][None, :])
    small[0:1, :] = s_ln2
    grad_mid[...] = up + back2
    hand_out(stage, keep, send)


def heads_back(qkv, probs, mix, dmix, dqkv):
    width = mix.shape[1]
    score_scale = HD ** (-0.5)
    per_group = LANES // HD
    for group in range(width // LANES):
        sums = None
        together = 4
        for first in range(group * per_group, (group + 1) * per_group, together):
            masks, deltas, dos = [], [], []
            for head in range(first, first + together):
                lo, sub, mine, q, k, v = head_columns(qkv, head, width)
                do = dmix[:, lo : lo + LANES]
                do_mine = jnp.where(mine, do, jnp.zeros_like(do))
                deltas.append(jnp.sum(do_mine.astype(F32) * mix[:, lo : lo + LANES], axis=-1, keepdims=True))
                masks.append(mine)
                dos.append(do_mine)
            rows = do.shape[0]
            prob = probs[first : first + together]
            dp = dot_last(jnp.concatenate(dos, axis=0), v).reshape(together, rows, rows)
            ds = (prob.astype(F32) * (dp - jnp.stack(deltas))).astype(BF16)
            dq = dot(ds.reshape(together * rows, rows), k).reshape(together, rows, LANES)
            for i, mine in enumerate(masks):
                parts = (dq[i] * score_scale, dot_first(ds[i], q) * score_scale, dot_first(prob[i], do))
                sums = parts if sums is None else [jnp.where(mine, a, b) for a, b in zip(parts, sums)]
        for i, part in enumerate(sums):
            dqkv[:, i * width + lo : i * width + lo + LANES] = part.astype(BF16)


def backward_kernel(
    me, small, grad_mid, normed1, inv1, qkv, probs, mix, gain1, w_qkv, w_proj,
    out_a, out_b, out_c, out_d, keep_t, send_t,
    dmix, dqkv, stage_t,
):
    width = mix.shape[1]
    pieces, rows, _ = stage_t.shape
    stage_t[:, rows - EXTRA :] = jnp.zeros((pieces, EXTRA, width), BF16)
    extra = [me[0] * (PIECES // 2) + low_slot(i, me, 1) for i in range(BLOCKS + 2)]
    for i in range(BLOCKS + 1):
        stage_t[extra[i + 1], rows - EXTRA : rows - EXTRA + 1] = small[i : i + 1, :].astype(BF16)
    grad_attn = grad_mid[...].astype(BF16)
    dmix[...] = dot_last(grad_attn, w_proj[...]).astype(BF16)
    heads_back(qkv, probs, mix, dmix, dqkv)
    grad_proj = dot_first(mix[...].astype(BF16), grad_attn).astype(BF16)
    put_block(stage_t, grad_proj, me, 1, 3 * width // PIECES)
    normed = normed1[...]
    h1 = (normed * gain1[...][None, :]).astype(BF16)
    grad = dot_first(h1, dqkv[...]).astype(BF16)
    for j in range(3):
        put_block(stage_t, grad[:, j * width : (j + 1) * width], me, 1, j * width // PIECES)
    t1 = dot_last(dqkv[...], w_qkv[...])
    back1, s_ln1 = norm_back(t1, normed, inv1[...], gain1[...][None, :])
    stage_t[extra[0], rows - EXTRA : rows - EXTRA + 1] = s_ln1.astype(BF16)
    hand_out(stage_t, keep_t, send_t)
    result = grad_mid[...] + back1
    quarter = result.shape[0] // 4
    for i, ref in enumerate((out_a, out_b, out_c, out_d)):
        ref[...] = result[i * quarter : (i + 1) * quarter].reshape(ref.shape).astype(BF16)


def finish_kernel(*refs):
    me, back_a, back_b, back_c, back_d = refs[:5]
    parts = refs[5:-15]
    out, g_ln1, g_qkv, g_proj, g_ln2, g_fc1, g_bfc1, g_fc2 = refs[-15:-7]
    out_near, fc1, fc2, qkv, proj, smalls, sems = refs[-7:]
    half = PIECES // 2
    width, ff = fc1.shape
    rows = width * BLOCKS // PIECES
    thin = width // PIECES
    half_x, half_y = out_near.shape[0] // 2, out_near.shape[1] // 2
    copies = []

    def leave(source, target):
        copies.append(pltpu.make_async_copy(source, target, sems.at[len(copies)]))
        copies[-1].start()

    out_near[half_x:, half_y:] = back_a[...]
    out_near[half_x:, :half_y] = back_b[...]
    out_near[:half_x, half_y:] = back_c[...]
    out_near[:half_x, :half_y] = back_d[...]
    leave(out_near, out)
    total = jnp.zeros((8, width), F32)
    for ref in parts:
        for j in range(ref.shape[0]):
            value = ref[j].astype(F32)
            total = total + jnp.sum((value * value).reshape(-1, 8, width), axis=0)
    total = jnp.sum(jnp.sum(total, axis=0, keepdims=True), axis=1, keepdims=True)
    factor = math.sqrt(param_count(width, ff)) * lax.rsqrt(total)
    per_block = PIECES // BLOCKS
    def spot(core, order, slot):
        piece = core * half + (slot ^ jnp.where(core == 0, me[1 + 2 * order], me[2 + 2 * order]))
        top = pl.multiple_of(piece % per_block * rows, rows)
        left = pl.multiple_of(piece // per_block * width, width)
        return piece, pl.ds(top, rows), pl.ds(left, width)

    for kind in range(3):
        for i, ref in enumerate(parts[4 * (kind // 2) : 4 * (kind // 2) + 4]):
            core = me[0] ^ (i // 2)
            for j in range(ref.shape[0]):
                slot = i % 2 * ref.shape[0] + j
                if kind == 0:
                    piece, _, _ = spot(core, 0, slot)
                    value = (ref[j, :rows].astype(F32) * factor).astype(BF16)
                    fc2[pl.ds(pl.multiple_of(piece * rows, rows), rows), :] = value
                elif kind == 1:
                    _, down, across = spot(core, 0, slot)
                    fc1[down, across] = (ref[j, rows:].astype(F32) * factor).astype(BF16)
                else:
                    value = ref[j].astype(F32) * factor
                    piece, down, across = spot(core, 1, slot)
                    for part in range(3):
                        at = slice(part * width, (part + 1) * width)
                        qkv[piece, :, at] = value[part * thin : (part + 1) * thin].astype(BF16)
                    proj[piece] = value[3 * thin : 4 * thin].astype(BF16)
                    smalls[piece] = value[4 * thin :]
        if kind == 0:
            leave(fc2, g_fc2)
        elif kind == 1:
            leave(fc1, g_fc1)
        else:
            leave(qkv, g_qkv)
            leave(proj, g_proj)
    g_ln1[...] = smalls[0, 0]
    g_ln2[...] = smalls[1, 0]
    for j in range(BLOCKS):
        g_bfc1[j * width : (j + 1) * width] = smalls[2 + j, 0]
    for copy in copies:
        copy.wait()


def param_count(width, ff):
    return 4 * width * width + 2 * width * ff + 2 * width + ff


VMEM = pl.BlockSpec(memory_space=pltpu.VMEM)
SMEM = pl.BlockSpec(memory_space=pltpu.SMEM)
HBM = pl.BlockSpec(memory_space=pltpu.HBM)


def shape(dims, dtype):
    return jax.ShapeDtypeStruct(dims, dtype)


def like(*arrays):
    return [pltpu.VMEM(a.shape, a.dtype) for a in arrays]


def call(kernel, outs, scratch, flops, me, near, far=(), out_specs=None):
    far = tuple(pltpu.with_memory_space_constraint(a, pltpu.HBM) for a in far)
    args = (me, *near, *far)
    moved = sum(a.size * a.dtype.itemsize for a in args) + sum(
        math.prod(o.shape) * o.dtype.itemsize for o in outs
    )
    return pl.pallas_call(
        kernel,
        out_shape=outs,
        in_specs=[SMEM] + [VMEM] * len(near) + [HBM] * len(far),
        out_specs=out_specs or (VMEM,) * len(outs),
        scratch_shapes=scratch,
        cost_estimate=pl.CostEstimate(flops=flops, bytes_accessed=moved, transcendentals=0),
        compiler_params=pltpu.CompilerParams(vmem_limit_bytes=KERNEL_VMEM),
    )(*args)


def neighbour(shard, step_x, step_y):
    size_x, size_y = lax.axis_size("gx"), lax.axis_size("gy")
    pairs = [
        (x * size_y + y, (x + step_x) % size_x * size_y + (y + step_y) % size_y)
        for x in range(size_x)
        for y in range(size_y)
    ]
    return lax.ppermute(shard, ("gx", "gy"), pairs)


def arriving(tile):
    half_x, half_y = tile.shape[1] // 2, tile.shape[2] // 2
    return (
        neighbour(tile[:, half_x:, :half_y], 0, -1),
        neighbour(tile[:, :half_x, half_y:], -1, 0),
        neighbour(tile[:, :half_x, :half_y], -1, -1),
    )


def window_codes(labels):
    tile_x, tile_y, tile_z = labels.shape
    half_x, half_y = tile_x // 2, tile_y // 2
    last_x = (lax.axis_index("gx") == lax.axis_size("gx") - 1).astype(jnp.int32)
    last_y = (lax.axis_index("gy") == lax.axis_size("gy") - 1).astype(jnp.int32)
    upper_x = (jnp.arange(tile_x) >= half_x).astype(jnp.int32)
    upper_y = (jnp.arange(tile_y) >= half_y).astype(jnp.int32)
    upper_z = (jnp.arange(tile_z) >= tile_z - WZ // 2).astype(jnp.int32)
    codes = (
        labels * 8
        + (4 * last_x) * upper_x[:, None, None]
        + (2 * last_y) * upper_y[None, :, None]
        + upper_z[None, None, :]
    )
    codes = jnp.roll(codes, WZ // 2, axis=2)
    parts = (
        codes[:half_x, :half_y], codes[:half_x, half_y:],
        codes[half_x:, :half_y], codes[half_x:, half_y:],
    )
    return jnp.concatenate([part.reshape(-1) for part in parts])


def swap(shard, flips):
    size_x, size_y = lax.axis_size("gx"), lax.axis_size("gy")
    pairs = [
        (x * size_y + y, (x ^ flips[y % 2][0]) * size_y + (y ^ flips[y % 2][1]))
        for x in range(size_x)
        for y in range(size_y)
    ]
    return lax.ppermute(shard, ("gx", "gy"), pairs)


def add(first, *others):
    total = first.astype(F32)
    for other in others:
        total = total + other.astype(F32)
    return total


SIDE, NEAR, LAYER = (0, 2), (1, 0), (2, 0)
CORE = ((0, 1), (0, 1))
SPARE = 4
ORDERS = (
    ((SIDE, LAYER), (NEAR, SIDE), (LAYER, NEAR)),
    ((NEAR, NEAR), (LAYER, LAYER), (SIDE, SIDE)),
)


def place():
    index_x, index_y = lax.axis_index("gx"), lax.axis_index("gy")
    numbers = [index_y % 2]
    for order in ORDERS:
        for core in range(2):
            number = jnp.int32(0)
            for flips in order:
                flip_x, flip_y = flips[core]
                bit = (index_x & flip_x) if flip_x else (index_y & flip_y)
                number = 2 * number + (bit != 0).astype(jnp.int32)
            numbers.append(number)
    return jnp.stack(numbers)


def fold(keep, got):
    half = keep.shape[0] // 2
    return (
        add(keep[:half], got[:half]).astype(BF16),
        add(keep[half:], got[half:]).astype(BF16),
    )


def after(values, first):
    return lax.optimization_barrier((*values, first))[: len(values)]


def spares():
    for axis in (0, 1):
        spare = SPARE
        while spare < lax.axis_size(("gx", "gy")[axis]):
            yield ((spare, 0) if axis == 0 else (0, spare),) * 2
            spare *= 2


def reduce_all(keep, send, got, keep_t, send_t, away):
    order, order_t = ORDERS
    got_t, = after([swap(send_t, CORE)], send)
    keep_t, send_t = fold(keep_t, got_t)
    homes, back = ((0, 1), (1, 0), (1, 1)), []
    for step in range(3):
        got_t = swap(send_t, order_t[step])
        if step < 2:
            got, home = after([got, neighbour(away[step], *homes[step])], send_t)
            back.append(home)
        else:
            got, = after([got], send_t)
        if step < 2:
            keep, send = fold(keep, got)
            got = swap(send, order[step + 1])
            got_t, = after([got_t], send)
            keep_t, send_t = fold(keep_t, got_t)
        else:
            low = add(keep[0], got[0]).astype(BF16)
            got_t, = after([got_t], low)
            low_t = add(keep_t[0], got_t[0]).astype(BF16)
    for flips in spares():
        got, got_t = swap(low, flips), swap(low_t, flips)
        if len(back) == 2:
            got, home = lax.optimization_barrier((got, neighbour(away[2], *homes[2])))
            back.append(home)
        low = add(low, after([got], low_t)[0]).astype(BF16)
        low_t = add(low_t, after([got_t], low)[0]).astype(BF16)
    parts, parts_t = low[None], low_t[None]
    for step in (2, 1, 0):
        more, more_t = swap(parts, order[step]), swap(parts_t, order_t[step])
        if step == 0:
            more, more_t = lax.optimization_barrier((more, more_t))
            break
        more, more_t = lax.optimization_barrier((more, more_t))
        parts, parts_t = jnp.concatenate([parts, more]), jnp.concatenate([parts_t, more_t])
    streams = ((parts, more), (parts_t, more_t))
    return back, [part for pair in streams for part in (*pair, swap(pair[0], CORE), swap(pair[1], CORE))]


def body(tokens, upstream, window_labels, ln1_gain, w_qkv, w_proj, ln2_gain, w_fc1, b_fc1, w_fc2):
    width, ff = w_fc1.shape
    heads = width // HD
    parts = arriving(jnp.stack([tokens, upstream]))
    codes = window_codes(window_labels)
    rows = codes.shape[0]
    me = place()
    piece = BLOCKS * width // PIECES
    thin = width // PIECES
    rows_f, rows_t = 2 * piece, 4 * thin + EXTRA
    half = shape((PIECES // 2, rows_f, width), BF16)
    half_t = shape((PIECES // 2, rows_t, width), BF16)
    weights = (w_qkv, w_proj)
    weights = call(
        fetch_kernel, tuple(shape(w.shape, BF16) for w in weights), [pltpu.SemaphoreType.DMA((2,))], 0, me, (), weights
    )
    w_qkv, w_proj = weights
    parts = after(parts, w_proj)
    keep, send, *saved = call(
        forward_kernel,
        (half, half)
        + (shape((1 + BLOCKS, width), F32), shape((rows, width), F32), shape((rows, width), F32), shape((rows, 1), F32))
        + (shape((rows, 3 * width), BF16), shape((heads, rows, rows), BF16), shape((rows, width), F32)),
        [pltpu.VMEM((rows, rows), F32), pltpu.VMEM((PIECES, rows_f, width), BF16), pltpu.VMEM((rows, ff), F32), pltpu.VMEM((rows, ff), F32), pltpu.VMEM((rows, ff), BF16), pltpu.VMEM((rows, ff), BF16)]
        + like(w_fc1, w_fc2)
        + [pltpu.SemaphoreType.DMA((2,))],
        2 * rows * width * (4 * width + 5 * ff) + 4 * heads * rows * rows * LANES,
        me,
        (tokens, upstream, *parts, codes[:, None], codes[None, :], ln1_gain, ln2_gain, b_fc1, w_qkv, w_proj),
        (w_fc1, w_fc2),
    )
    quarter = shape(parts[0].shape[1:], BF16)
    small, grad_mid, normed1, inv1, qkv, probs, mix = saved
    got = swap(send, CORE)
    *done, keep_t, send_t = call(
        backward_kernel,
        (quarter,) * 4 + (half_t, half_t),
        [
            pltpu.VMEM((rows, width), BF16),
            pltpu.VMEM((rows, 3 * width), BF16),
            pltpu.VMEM((PIECES, rows_t, width), BF16),
        ],
        2 * rows * width * 8 * width + 8 * heads * rows * rows * LANES,
        me,
        (small, grad_mid, normed1, inv1, qkv, probs, mix, ln1_gain, w_qkv, w_proj),
    )
    got, = after([got], keep_t)
    keep, send = fold(keep, got)
    got = swap(send, ORDERS[0][0])
    back, slots = reduce_all(keep, send, got, keep_t, send_t, done[1:])
    result, g_ln1, g_qkv, g_proj, g_ln2, g_fc1, g_bfc1, g_fc2 = call(
        finish_kernel,
        (
            shape(tokens.shape, BF16), shape((width,), F32), shape((PIECES, thin, 3 * width), BF16),
            shape((PIECES, thin, width), BF16), shape((width,), F32), shape((width, ff), BF16),
            shape((ff,), F32), shape((ff, width), BF16),
        ),
        like(tokens, w_fc1, w_fc2)
        + [
            pltpu.VMEM((PIECES, thin, 3 * width), BF16),
            pltpu.VMEM((PIECES, thin, width), BF16),
            pltpu.VMEM((PIECES, EXTRA, width), F32),
            pltpu.SemaphoreType.DMA((5,)),
        ],
        4 * width * width,
        me,
        (done[0], *back, *slots),
        out_specs=(HBM, VMEM, HBM, HBM, VMEM, HBM, VMEM, HBM),
    )
    g_qkv, g_proj = g_qkv.reshape(width, 3 * width), g_proj.reshape(width, width)
    return (result, g_ln1, g_qkv, g_proj, g_ln2, g_fc1, g_bfc1, g_fc2)


def solution(mesh):
    return jax.shard_map(
        body,
        mesh=mesh,
        in_specs=(
            P("gx", "gy", None, None),
            P("gx", "gy", None, None),
            P("gx", "gy", None),
            P(), P(), P(), P(), P(), P(), P(),
        ),
        out_specs=(P("gx", "gy", None, None), P(), P(), P(), P(), P(), P(), P()),
        check_vma=False,
    )
```
